256 devices in a mesh: band: 64 (over y, z, core), lev: 4 (over x).
Axes of the slice: x: 4, y: 4, z: 8, core: 2. Of those that a mesh axis runs over, the one named last changes fastest.
Arguments:
- spectral: float32 [5376, 16, 128], P('band', 'lev'), may hold values from -6 to 6
- legendre: bfloat16 [5376, 64, 1024], P('band'), may hold values from -0.15625 to 0.15625
- wave_ids: int32 [512], P('band'), may hold values from 0 to 1279, as said below
- block_slot: int32 [5376], P('band'), may hold values from 0 to 7, as said below
- block_start: int32 [5376], P('band'), may hold values from 0 to 1216, as said below
- lat_weights: float32 [1024], replicated, may hold values from 0.5 to 2
- drag: float32 [16, 2, 1024], P('lev'), may hold values from 0.1 to 1
- mode_inverse: float32 [16, 16], replicated, may hold values from -1.5 to 1.5
- level_modes: float32 [16, 16], replicated, may hold values from -1.5 to 1.5
- depths: float32 [16], replicated, may hold values from 0.1 to 3
Outputs:
- spectral_next: float32 [5376, 16, 128], P('band', 'lev')
The draws below stay inside these ranges and needn't reach their ends.
Inputs may be any that keep to these rules, and one draw needn't show every extreme that they name: `wave_ids`: distinct wavenumbers. The slots of index b of band, entries b * 8 to (b + 1) * 8 - 1, hold 4 pairs m and 1279 - m in some order; the pair 0 and 1279 is always present. `block_slot`: blocks b * 84 to (b + 1) * 84 - 1 belong to index b of band. For each slot of index b with wavenumber m there is exactly one block with each start 0, 64, 128, ... below 1280 - m, and no other block; the blocks stand in no particular order. `block_start`: A multiple of 64; see block_slot.
All inputs are finite; a program needn't handle non-finite values.
Results may differ from the reference program's by a relative error of at most 0.009.
Values may be sent and summed in bfloat16 or wider, within the bound.
No kernel may reach another device: no remote copies, remote signals or barrier semaphores. Data moves between devices by JAX's collectives and lax.ppermute only.
A program may use at most 128 MiB of HBM per device.

```python
import math
import jax
import jax.numpy as jnp
from jax import lax

NTRUNC = 1280
NLON = 4096
LEV = 16
BLK = 64
WAVE_DEV = 8
WAVES = 512
BLK_DEV = 84
BLOCKS = 5376
NLAT_H = 1024


def pair_layout(key):
    base_key = jax.random.fold_in(key, 1729)
    device_count = WAVES // WAVE_DEV
    pair_count = WAVES // 2
    others = jax.random.permutation(jax.random.fold_in(base_key, 1), NTRUNC // 2 - 1).astype(jnp.int32) + 1
    low_waves = jnp.concatenate([jnp.zeros((1,), jnp.int32), others[:pair_count - 1]])
    low_waves = jax.random.permutation(jax.random.fold_in(base_key, 2), low_waves)
    high_waves = NTRUNC - 1 - low_waves
    owned = jnp.stack([low_waves, high_waves], axis=1).reshape(device_count, WAVE_DEV)
    device_keys = jax.random.split(jax.random.fold_in(base_key, 3), device_count)
    owned = jax.vmap(jax.random.permutation)(device_keys, owned)
    block_counts = (NTRUNC - owned + BLK - 1) // BLK
    block_ends = jnp.cumsum(block_counts, axis=1)
    begins = block_ends - block_counts
    positions = jnp.arange(BLK_DEV, dtype=jnp.int32)
    slot_of = jnp.sum((block_ends[:, None, :] <= positions[None, :, None]).astype(jnp.int32), axis=2)
    start_of = (positions[None, :] - jnp.take_along_axis(begins, slot_of, axis=1)) * BLK
    shuffle_keys = jax.random.split(jax.random.fold_in(base_key, 4), device_count)
    shuffle = jax.vmap(jax.random.permutation)(shuffle_keys, jnp.broadcast_to(positions, (device_count, BLK_DEV)))
    slot_of = jnp.take_along_axis(slot_of, shuffle, axis=1)
    start_of = jnp.take_along_axis(start_of, shuffle, axis=1)
    return (owned.reshape(WAVES).astype(jnp.int32), slot_of.reshape(device_count * BLK_DEV).astype(jnp.int32), start_of.reshape(device_count * BLK_DEV).astype(jnp.int32))


def draw_wave_ids(key, part):
    return pair_layout(key)[0]


def draw_block_slot(key, part):
    return pair_layout(key)[1]


def draw_block_start(key, part):
    return pair_layout(key)[2]


def levels(own_key, dims, cuts, least, top_value):
    loudness = 1.0
    for axis_at, shards_of in cuts:
        steps = jax.random.uniform(jax.random.fold_in(jax.random.fold_in(own_key, 6), axis_at), (shards_of,), jnp.float32, least / len(cuts), top_value / len(cuts))
        loudness = loudness * jnp.repeat(jnp.exp(steps), dims[axis_at] // shards_of).reshape((-1,) + (1,) * (len(dims) - 1 - axis_at))
    return loudness


def normal_values(stream_key, extent, width, bound, cuts=(), held_as=jnp.bfloat16):
    values = jax.random.normal(stream_key, extent, jnp.float32) * width
    if len(cuts) > 0:
        values = levels(stream_key, extent, cuts, -0.22, 0.18) * values
    return jnp.clip(values, min=-bound, max=bound).astype(held_as)


def setup_inputs(seed: int = 0) -> dict:
    key_list = jax.random.split(jax.random.key(seed), 11)
    spectral = normal_values(key_list[0], (BLOCKS, LEV, 2 * BLK), 1.0, 6.0, ((0, 64), (1, 4)), jnp.float32)
    legendre = normal_values(key_list[1], (BLOCKS, BLK, NLAT_H), NTRUNC ** -0.5, 0.15625, ((0, 64),))
    wave_ids = draw_wave_ids(jax.random.fold_in(key_list[10], 71), 0)
    block_slot = draw_block_slot(jax.random.fold_in(key_list[10], 71), 0)
    block_start = draw_block_start(jax.random.fold_in(key_list[10], 71), 0)
    lat_weights = jnp.clip(jnp.exp(jax.random.uniform(key_list[5], (NLAT_H,), jnp.float32, math.log(0.5), math.log(2.0))), 0.5, 2.0)
    drag = jnp.clip(jnp.exp(math.log(1.0) - 2.3025851 * jax.random.uniform(key_list[6], (LEV, 2, NLAT_H), jnp.float32) ** levels(key_list[6], (LEV, 2, NLAT_H), ((0, 4),), -0.2, 0.2)), 0.1, 1.0)
    mode_inverse = normal_values(key_list[7], (LEV, LEV), LEV ** -0.5, 1.5, (), jnp.float32)
    level_modes = normal_values(key_list[8], (LEV, LEV), LEV ** -0.5, 1.5, (), jnp.float32)
    depths = jnp.clip(jnp.exp(jax.random.uniform(key_list[9], (LEV,), jnp.float32, math.log(0.1), math.log(3.0))), 0.1, 3.0)
    return {"spectral": spectral, "legendre": legendre, "wave_ids": wave_ids, "block_slot": block_slot, "block_start": block_start, "lat_weights": lat_weights, "drag": drag, "mode_inverse": mode_inverse, "level_modes": level_modes, "depths": depths}


def row_offsets(row_count):
    half_rows = row_count // 2
    positions = jnp.arange(row_count, dtype=jnp.int32)
    return jnp.where(positions < half_rows, 2 * positions, 2 * (positions - half_rows) + 1)

def reference(spectral, legendre, wave_ids, block_slot, block_start, lat_weights, drag, mode_inverse, level_modes, depths):
    half_rows = BLK // 2
    groups = BLOCKS // BLK_DEV
    owner = jnp.arange(BLOCKS, dtype=jnp.int32) // BLK_DEV * WAVE_DEV + block_slot
    wave_of_block = jnp.take(wave_ids, owner)
    degree = wave_of_block[:, None] + block_start[:, None] + row_offsets(BLK)[None, :]
    live_rows = (degree < NTRUNC).astype(jnp.float32)
    live_cols = jnp.concatenate([live_rows, live_rows], axis=1)
    masked = spectral * live_cols[:, None, :]
    coeff = masked.astype(jnp.bfloat16)
    local_slots = jnp.arange(WAVE_DEV, dtype=jnp.int32)
    highest = lax.Precision.HIGHEST

    def inverse_group(pieces):
        group_coeff, group_legendre, group_slots = pieces
        split_coeff = group_coeff.astype(jnp.float32).reshape(BLK_DEV, LEV, 2, 2, half_rows)
        wide_legendre = group_legendre.astype(jnp.float32)
        even_part = jnp.einsum('klcr,kri->klci', split_coeff[:, :, :, 0, :], wide_legendre[:, :half_rows, :], precision=highest)
        odd_part = jnp.einsum('klcr,kri->klci', split_coeff[:, :, :, 1, :], wide_legendre[:, half_rows:, :], precision=highest)
        hemispheres = jnp.stack([even_part + odd_part, even_part - odd_part], axis=3)
        matches = (group_slots[:, None] == local_slots[None, :]).astype(jnp.float32)
        return jnp.einsum('ks,klchi->slchi', matches, hemispheres, precision=highest)
    fourier = lax.map(inverse_group, (coeff.reshape(groups, BLK_DEV, LEV, 2 * BLK), legendre.reshape(groups, BLK_DEV, BLK, NLAT_H), block_slot.reshape(groups, BLK_DEV)))
    fourier = fourier.reshape(WAVES, LEV, 2, 2, NLAT_H).astype(jnp.bfloat16)
    spectrum_len = NLON // 2 + 1
    real_scale = jnp.where(wave_ids == 0, NLON * 1.0, NLON * 0.5).astype(jnp.float32) / math.sqrt(WAVES)
    imag_scale = jnp.where(wave_ids == 0, 0.0, NLON * 0.5).astype(jnp.float32) / math.sqrt(WAVES)

    def grid_level(level_fourier):
        values = level_fourier.astype(jnp.float32)
        real_part = jnp.zeros((spectrum_len, 2, NLAT_H), jnp.float32).at[wave_ids].set(values[:, 0] * real_scale[:, None, None])
        imag_part = jnp.zeros((spectrum_len, 2, NLAT_H), jnp.float32).at[wave_ids].set(values[:, 1] * imag_scale[:, None, None])
        grid_values = jnp.fft.irfft(lax.complex(real_part, imag_part), n=NLON, axis=0)
        drag_force = grid_values * jnp.abs(grid_values)
        spectrum = jnp.fft.rfft(drag_force, axis=0)[wave_ids] / math.sqrt(NLON)
        return jnp.stack([jnp.real(spectrum), jnp.imag(spectrum)], axis=1).astype(jnp.bfloat16)
    drag_spec = lax.map(grid_level, jnp.moveaxis(fourier, 1, 0))
    drag_spec = jnp.moveaxis(drag_spec, 0, 1)
    northern = drag_spec[:, :, :, 0, :].astype(jnp.float32)
    southern = drag_spec[:, :, :, 1, :].astype(jnp.float32)
    drag_north = drag[:, 0, :][None, :, None, :]
    drag_south = drag[:, 1, :][None, :, None, :]
    weights_grid = lat_weights[None, None, None, :]
    symmetric = (-weights_grid * (drag_north * northern + drag_south * southern)).astype(jnp.bfloat16)
    antisymmetric = (-weights_grid * (drag_north * northern - drag_south * southern)).astype(jnp.bfloat16)
    degree_f = degree.astype(jnp.float32)
    growth = degree_f * (degree_f + 1.0) / (NTRUNC * NTRUNC)
    growth = jnp.concatenate([growth, growth], axis=1)

    def direct_group(pieces):
        group_legendre, group_slots, group_sym, group_anti, group_masked, group_live, group_growth = pieces
        wide_legendre = group_legendre.astype(jnp.float32)
        sym_blocks = jnp.take(group_sym, group_slots, axis=0).astype(jnp.float32)
        anti_blocks = jnp.take(group_anti, group_slots, axis=0).astype(jnp.float32)
        even_part = jnp.einsum('klci,kri->klcr', sym_blocks, wide_legendre[:, :half_rows, :], precision=highest)
        odd_part = jnp.einsum('klci,kri->klcr', anti_blocks, wide_legendre[:, half_rows:, :], precision=highest)
        tendency = jnp.stack([even_part, odd_part], axis=3).reshape(BLK_DEV, LEV, 2 * BLK) * group_live[:, None, :]
        combined = group_masked + tendency
        modal = jnp.einsum('al,klx->kax', mode_inverse, combined, precision=highest)
        implicit_gain = 1.0 / (1.0 + depths[None, :, None] * group_growth[:, None, :])
        return jnp.einsum('la,kax->klx', level_modes, modal * implicit_gain, precision=highest)
    result = lax.map(direct_group, (legendre.reshape(groups, BLK_DEV, BLK, NLAT_H), block_slot.reshape(groups, BLK_DEV), symmetric.reshape(groups, WAVE_DEV, LEV, 2, NLAT_H), antisymmetric.reshape(groups, WAVE_DEV, LEV, 2, NLAT_H), masked.reshape(groups, BLK_DEV, LEV, 2 * BLK), live_cols.reshape(groups, BLK_DEV, 2 * BLK), growth.reshape(groups, BLK_DEV, 2 * BLK)))
    return result.reshape(BLOCKS, LEV, 2 * BLK)
```

```python
import math

import jax
import jax.numpy as jnp
from jax import lax
from jax.experimental import pallas as pl
from jax.experimental.pallas import tpu as pltpu
from jax.sharding import PartitionSpec as P

NTRUNC = 1280
NLON = 4096
BLOCKS = 84
ROWS = 64
LATS = 1024
LEVELS = 4
ALL_LEVELS = 16
SOURCES = 64
SENT_ROWS = 24
CHUNK = 12
CHUNKS = BLOCKS // CHUNK
KPAD = 96
XPAD = 1152
XTILES = XPAD // 128
F32 = jnp.float32
BF16 = jnp.bfloat16
MB = 1024 * 1024


def iota(shape, dim):
    return lax.broadcasted_iota(jnp.int32, shape, dim)


def row_offset(lane):
    r = lane % ROWS
    half = ROWS // 2
    return jnp.where(r < half, 2 * r, 2 * (r - half) + 1)


def sincos(turns):
    quarter = ((turns + 512) >> 10) & 3
    rest = ((turns + 512) & 1023) - 512
    t = rest.astype(F32) * (2.0 * math.pi / NLON)
    z = t * t
    s = t * (1.0 + z * (-1.0 / 6 + z * (1.0 / 120 + z * (-1.0 / 5040 + z * (1.0 / 362880)))))
    c = 1.0 + z * (-0.5 + z * (1.0 / 24 + z * (-1.0 / 720 + z * (1.0 / 40320))))
    swap = (quarter & 1) == 1
    cos = jnp.where(swap, s, c)
    sin = jnp.where(swap, c, s)
    cos = jnp.where((quarter == 1) | (quarter == 2), -cos, cos)
    sin = jnp.where(quarter >= 2, -sin, sin)
    return cos, sin


def forward_kernel(
    pos_ref, base_ref, even_ref, lev_ref, spec_ref, mode_ref, leg_ref,
    out_ref, legv_ref, growth_ref, kron_ref, lhs_ref, acc_ref, sems,
):
    copies = [
        pltpu.make_async_copy(
            leg_ref.at[pl.ds(c * CHUNK, CHUNK)], legv_ref.at[pl.ds(c * CHUNK, CHUNK)], sems.at[c]
        )
        for c in range(CHUNKS)
    ]
    for copy in copies:
        copy.start()
    lane = iota((8, 128), 1)
    sub = iota((8, 128), 0)
    offset = row_offset(lane)
    left = lane < 64
    upper = sub < 4
    sign = jnp.where(lane % ROWS < ROWS // 2, 1.0, -1.0).astype(F32)

    def build(j, carry):
        k0 = 2 * j
        degree = jnp.where(upper, base_ref[k0], base_ref[k0 + 1]) + offset
        own = spec_ref[pl.ds(pl.multiple_of(8 * j, 8), 8), :]
        own = jnp.where(degree < NTRUNC, own, 0.0)
        turned = pltpu.roll(own, 64, 1)
        parts = (
            jnp.where(left, own, pltpu.roll(turned, 4, 0)),
            jnp.where(left, turned, pltpu.roll(own, 4, 0)),
        )
        match = jnp.where(left, pos_ref[k0], pos_ref[k0 + 1]) == sub
        where = pl.ds(pl.multiple_of(128 * j, 128), 128)
        for l in range(LEVELS):
            north = jnp.concatenate(
                [
                    jnp.where(match, jnp.broadcast_to(p[l : l + 1], (8, 128)), 0.0)
                    for p in parts
                ],
                axis=0,
            )
            south = north * jnp.concatenate([sign, sign], axis=0)
            lhs_ref[32 * l : 32 * l + 16, where] = north.astype(BF16)
            lhs_ref[32 * l + 16 : 32 * l + 32, where] = south.astype(BF16)
        return carry

    lax.fori_loop(0, BLOCKS // 2, build, 0, unroll=6)

    growth_ref[...] = jnp.zeros_like(growth_ref)
    one = row_offset(iota((1, 128), 1))

    def grow(k, carry):
        degree = (base_ref[k] + one).astype(F32)
        growth_ref[pl.ds(k, 1), :] = degree * (degree + 1.0) / (NTRUNC * NTRUNC)
        return carry

    lax.fori_loop(0, BLOCKS, grow, 0, unroll=12)
    lev = lev_ref[0]
    row_pick = (iota((256, ALL_LEVELS), 0) // 16 == iota((256, ALL_LEVELS), 1)).astype(F32)
    col = iota((ALL_LEVELS, 256), 1) // 16
    source_level = ((lev - col // LEVELS) & 3) * LEVELS + col % LEVELS
    col_pick = (iota((ALL_LEVELS, 256), 0) == source_level).astype(F32)
    high = lax.Precision.HIGHEST
    wide = jnp.dot(jnp.dot(row_pick, mode_ref[...], precision=high), col_pick, precision=high)
    wide = jnp.where(iota((256, 256), 0) % 16 == iota((256, 256), 1) % 16, wide, 0.0)
    wide_high = wide.astype(BF16)
    kron_ref[:, 0:256] = wide_high
    kron_ref[:, 256:512] = (wide - wide_high.astype(F32)).astype(BF16)

    for c in range(CHUNKS):
        copies[c].wait()
        lhs = lhs_ref[:, c * CHUNK * ROWS : (c + 1) * CHUNK * ROWS]
        for n in range(LATS // 256):
            cols = slice(256 * n, 256 * n + 256)
            rhs = legv_ref[c * CHUNK : (c + 1) * CHUNK, :, cols].reshape(CHUNK * ROWS, 256)
            part = jnp.dot(lhs, rhs, preferred_element_type=F32)
            if c == 0:
                acc_ref[:, cols] = part
            else:
                acc_ref[:, cols] += part
    ids = jnp.zeros((8, 128), jnp.int32)
    for p in range(4):
        ids = jnp.where(sub == p, even_ref[p] >> 4, ids)
        ids = jnp.where(sub == 4 + p, even_ref[p] & 15, ids)
    ids = ids.astype(F32).astype(BF16)
    for g in range(8):
        for b in range(8):
            out_ref[8 * g + b, 0:16, :] = acc_ref[
                16 * g : 16 * g + 16, 128 * b : 128 * b + 128
            ].astype(BF16)
            out_ref[8 * g + b, 16:24, :] = ids


def grid_kernel(in_ref, out_ref, recv_ref, tw_ref, g_ref, send_ref):
    recv_ref[...] = in_ref[...].astype(F32).reshape(SOURCES * SENT_ROWS, 128)

    def rows_of(j):
        return recv_ref[pl.ds(j, SOURCES, stride=SENT_ROWS), :]

    lane = iota((32, 128), 1)
    lane8 = iota((8, 128), 1)
    shift = [sincos(((NTRUNC - 1) * (128 * a + lane8)) & (NLON - 1)) for a in range(XTILES)]

    for p in range(4):
        whole = (rows_of(16 + p) * 16.0 + rows_of(20 + p)).astype(jnp.int32)
        for half in range(2):
            wave = whole[32 * half : 32 * half + 32]
            rows = slice(64 * p + 32 * half, 64 * p + 32 * half + 32)
            cos, sin = sincos((wave * lane) & (NLON - 1))
            step_cos, step_sin = sincos((wave * 128) & (NLON - 1))
            for a in range(XTILES):
                cols = slice(128 * a, 128 * a + 128)
                c1 = jnp.concatenate([shift[a][0]] * 4, axis=0)
                s1 = jnp.concatenate([shift[a][1]] * 4, axis=0)
                tw_ref[0, rows, cols] = cos.astype(BF16)
                tw_ref[1, rows, cols] = sin.astype(BF16)
                tw_ref[2, rows, cols] = (c1 * cos + s1 * sin).astype(BF16)
                tw_ref[3, rows, cols] = (s1 * cos - c1 * sin).astype(BF16)
                if a + 1 < XTILES:
                    cos, sin = cos * step_cos - sin * step_sin, sin * step_cos + cos * step_sin

    first_row = (0, 8, 4, 12)
    spectra = [
        jnp.concatenate([rows_of(f + p) for p in range(4)], axis=0).T.astype(BF16)
        for f in first_row
    ]
    for a in range(XTILES):
        cols = slice(128 * a, 128 * a + 128)
        ce, se, co, so = [
            jnp.dot(spectra[i], tw_ref[i, :, cols], preferred_element_type=F32) for i in range(4)
        ]
        minus, plus = ce - se, ce + se
        odd_minus, odd_plus = co - so, co + so
        f1, f2, f3, f4 = [
            v * jnp.abs(v)
            for v in (minus + odd_minus, minus - odd_minus, plus + odd_plus, plus - odd_plus)
        ]
        s12, d12, s34, d34 = f1 + f2, f1 - f2, f3 + f4, f3 - f4
        folded = (s12 + s34, s12 - s34, d12 + d34, d12 - d34)
        if a == 0:
            share = jnp.where(iota((1, 128), 1) == 0, 0.5, 1.0)
        else:
            share = jnp.where(iota((1, 128), 1) == 0, 0.5, 0.0)
        for i in range(4):
            value = folded[i]
            if a in (0, XTILES - 1):
                value = value * share
            g_ref[i, :, cols] = value.astype(BF16)
    scale = 1.0 / (512.0 * 64.0)
    for i in range(4):
        total = lax.dot_general(
            tw_ref[i], g_ref[i], (((1,), (1,)), ((), ())), preferred_element_type=F32
        )
        total = total * (scale if i % 2 == 0 else -scale)
        for p in range(4):
            send_ref[pl.ds(first_row[i] + p, SOURCES, stride=16), :] = total[64 * p : 64 * p + 64]
    out_ref[...] = send_ref[...].reshape(SOURCES, 16, 128).astype(BF16)


def direct_kernel(
    pos_ref, base_ref, arrived_ref, weight_ref, drag_ref, spec_ref, legv_ref,
    out_ref, v_ref, acc_ref, comb_ref,
):
    for b in range(8):
        cols = slice(128 * b, 128 * b + 128)
        weight = -weight_ref[0:1, cols]
        sides = []
        for l in range(LEVELS):
            north = (weight * drag_ref[l, 0:1, cols]) * arrived_ref[16 * l + b].astype(F32)
            south = (weight * drag_ref[l, 1:2, cols]) * arrived_ref[16 * l + 8 + b].astype(F32)
            sides.append((north + south, north - south))
        for a in range(2):
            for c in range(2):
                for pair in range(2):
                    piece = jnp.concatenate(
                        [sides[2 * pair + i][a][8 * c : 8 * c + 8] for i in range(2)], axis=0
                    )
                    row = (a * 2 + c) * 32 + pair * 16
                    v_ref[row : row + 16, cols] = piece.astype(BF16)
    comb_ref[...] = jnp.zeros_like(comb_ref)
    lane = iota((8, 128), 1)
    offset = row_offset(iota((4, 128), 1))
    left = lane < 64
    even_rows = lane % ROWS < ROWS // 2

    def one_group(group, carry):
        rhs = legv_ref[pl.ds(4 * group, 4)].reshape(4 * ROWS, LATS)
        product = lax.dot_general(
            v_ref[...], rhs, (((1,), (1,)), ((), ())), preferred_element_type=F32
        )
        acc_ref[0:128, :] = product[:, 0:128]
        acc_ref[128:256, :] = product[:, 128:256]
        for q in range(4):
            k = 4 * group + q
            rows = acc_ref[pl.ds(128 * (q // 2) + pos_ref[k], 16, stride=8), :]
            value = jnp.where(even_rows, rows[0:8], rows[8:16])
            if q % 2 == 0:
                value = jnp.where(left, value, pltpu.roll(pltpu.roll(value, 64, 1), 4, 0))
            else:
                value = jnp.where(left, pltpu.roll(value, 64, 1), pltpu.roll(value, 4, 0))
            total = value[0:4] + spec_ref[pl.ds(4 * k, 4), :]
            total = jnp.where(base_ref[k] + offset < NTRUNC, total, 0.0)
            comb_ref[pl.ds(k, 4, stride=KPAD), :] = total
        return carry

    lax.fori_loop(0, BLOCKS // 4, one_group, 0, unroll=3)
    out_ref[...] = comb_ref[...].astype(BF16)


def vertical_kernel(
    lev_ref, level_ref, depth_ref, own_ref, one_ref, two_ref, three_ref, growth_ref, kron_ref,
    out_ref,
):
    lev = lev_ref[0]
    sources = (own_ref, one_ref, two_ref, three_ref)
    for t in range(KPAD // 16):
        stacked = jnp.concatenate(
            [
                s[KPAD * j + 16 * t : KPAD * j + 16 * t + 16, :]
                for s in sources
                for j in range(LEVELS)
            ],
            axis=0,
        )
        modal = jnp.dot(kron_ref[:, 0:256], stacked, preferred_element_type=F32) + jnp.dot(
            kron_ref[:, 256:512], stacked, preferred_element_type=F32
        )
        growth = growth_ref[16 * t : 16 * t + 16, :]
        results = [None] * LEVELS
        for a in range(ALL_LEVELS):
            scaled = modal[16 * a : 16 * a + 16] / (1.0 + depth_ref[a] * growth)
            for l in range(LEVELS):
                term = level_ref[lev * LEVELS + l, a] * scaled
                results[l] = term if a == 0 else results[l] + term
        count = min(16, BLOCKS - 16 * t)
        for l in range(LEVELS):
            out_ref[pl.ds(64 * t + l, count, stride=LEVELS), :] = results[l][0:count]


def specs(*kinds):
    spaces = {"s": pltpu.SMEM, "v": pltpu.VMEM, "h": pl.ANY}
    return [pl.BlockSpec(memory_space=spaces[k]) for k in kinds]


def on_device(
    spectral, legendre, wave_ids, block_slot, block_start, lat_weights, drag, mode_inverse,
    level_modes, depths,
):
    odd = wave_ids % 2
    key = jnp.where(odd == 1, NTRUNC + (NTRUNC - 1 - wave_ids), wave_ids)
    place = jnp.sum((key[None, :] < key[:, None]).astype(jnp.int32), axis=1)
    slots = jnp.arange(8, dtype=jnp.int32)
    match = block_slot[:, None] == slots[None, :]
    pos = jnp.sum(jnp.where(match, place[None, :], 0), axis=1)
    base = jnp.sum(jnp.where(match, wave_ids[None, :], 0), axis=1) + block_start
    evens = jnp.sum(jnp.where(place[None, :] == slots[:4, None], wave_ids[None, :], 0), axis=1)
    lev = lax.axis_index("lev").astype(jnp.int32).reshape(1)
    spec = spectral.reshape(BLOCKS * LEVELS, 128)

    outgoing, legv, growth, kron = pl.pallas_call(
        forward_kernel,
        in_specs=specs("s", "s", "s", "s", "v", "v", "h"),
        out_specs=specs("v", "v", "v", "v"),
        out_shape=(
            jax.ShapeDtypeStruct((SOURCES, SENT_ROWS, 128), BF16),
            pltpu.VMEM((BLOCKS, ROWS, LATS), BF16),
            jax.ShapeDtypeStruct((KPAD, 128), F32),
            jax.ShapeDtypeStruct((256, 512), BF16),
        ),
        scratch_shapes=[
            pltpu.VMEM((128, BLOCKS * ROWS), BF16),
            pltpu.VMEM((128, LATS), F32),
            pltpu.SemaphoreType.DMA((CHUNKS,)),
        ],
        compiler_params=pltpu.CompilerParams(vmem_limit_bytes=32 * MB),
        name="forward",
    )(pos, base, evens, lev, spec, mode_inverse, legendre)
    incoming = lax.all_to_all(outgoing, "band", split_axis=0, concat_axis=0, tiled=True)
    filtered = pl.pallas_call(
        grid_kernel,
        in_specs=specs("v"),
        out_specs=specs("v")[0],
        out_shape=jax.ShapeDtypeStruct((SOURCES, 16, 128), BF16),
        scratch_shapes=[
            pltpu.VMEM((SOURCES * SENT_ROWS, 128), F32),
            pltpu.VMEM((4, 256, XPAD), BF16),
            pltpu.VMEM((4, 128, XPAD), BF16),
            pltpu.VMEM((SOURCES * 16, 128), F32),
        ],
        compiler_params=pltpu.CompilerParams(vmem_limit_bytes=24 * MB),
        name="grid",
    )(incoming)
    arrived = lax.all_to_all(filtered, "band", split_axis=0, concat_axis=0, tiled=True)
    combined = pl.pallas_call(
        direct_kernel,
        in_specs=specs("s", "s", "v", "v", "v", "v", "v"),
        out_specs=specs("v")[0],
        out_shape=jax.ShapeDtypeStruct((LEVELS * KPAD, 128), BF16),
        scratch_shapes=[
            pltpu.VMEM((128, LATS), BF16),
            pltpu.VMEM((256, 128), F32),
            pltpu.VMEM((LEVELS * KPAD, 128), F32),
        ],
        compiler_params=pltpu.CompilerParams(vmem_limit_bytes=32 * MB),
        name="direct",
    )(pos, base, arrived, lat_weights.reshape(1, LATS), drag, spec, legv)
    others = [
        lax.ppermute(combined, "lev", [(i, (i + s) % 4) for i in range(4)]) for s in (1, 2, 3)
    ]
    result = pl.pallas_call(
        vertical_kernel,
        in_specs=specs("s", "s", "s", "v", "v", "v", "v", "v", "v"),
        out_specs=specs("v")[0],
        out_shape=jax.ShapeDtypeStruct((BLOCKS * LEVELS, 128), F32),
        compiler_params=pltpu.CompilerParams(vmem_limit_bytes=16 * MB),
        name="vertical",
    )(lev, level_modes, depths, combined, *others, growth, kron)
    return result.reshape(BLOCKS, LEVELS, 128)


def solution(mesh):
    placed = (
        P("band", "lev", None),
        P("band", None, None),
        P("band"),
        P("band"),
        P("band"),
        P(),
        P("lev", None, None),
        P(),
        P(),
        P(),
    )
    return jax.shard_map(
        on_device, mesh=mesh, in_specs=placed, out_specs=P("band", "lev", None), check_vma=False
    )
```

```python
import math

import jax
import jax.numpy as jnp
from jax import lax
from jax.experimental import pallas as pl
from jax.experimental.pallas import tpu as pltpu
from jax.sharding import PartitionSpec as P

NTRUNC = 1280
NLON = 4096
BLOCKS = 84
ROWS = 64
LATS = 1024
LEVELS = 4
ALL_LEVELS = 16
SOURCES = 64
SENT_ROWS = 18
CHUNK = 12
CHUNKS = BLOCKS // CHUNK
KPAD = 88
XPAD = 1152
XTILES = XPAD // 128
F32 = jnp.float32
BF16 = jnp.bfloat16
MB = 1024 * 1024


def iota(shape, dim):
    return lax.broadcasted_iota(jnp.int32, shape, dim)


def row_offset(lane):
    r = lane % ROWS
    half = ROWS // 2
    return jnp.where(r < half, 2 * r, 2 * (r - half) + 1)


def sincos(turns):
    quarter = ((turns + 512) >> 10) & 3
    rest = ((turns + 512) & 1023) - 512
    t = rest.astype(F32) * (2.0 * math.pi / NLON)
    z = t * t
    s = t * (1.0 + z * (-1.0 / 6 + z * (1.0 / 120 + z * (-1.0 / 5040 + z * (1.0 / 362880)))))
    c = 1.0 + z * (-0.5 + z * (1.0 / 24 + z * (-1.0 / 720 + z * (1.0 / 40320))))
    swap = (quarter & 1) == 1
    cos = jnp.where(swap, s, c)
    sin = jnp.where(swap, c, s)
    cos = jnp.where((quarter == 1) | (quarter == 2), -cos, cos)
    sin = jnp.where(quarter >= 2, -sin, sin)
    return cos, sin


def forward_kernel(
    wave_hbm, slot_hbm, start_hbm, spec_hbm, leg_hbm,
    out_ref, legv_ref, masked_ref, pos_hbm, base_hbm,
    wave_ref, slot_ref, start_ref, place_ref, pos_ref, base_ref, lhs_ref, acc_ref, send_ref,
    sems, small,
):
    inputs = [
        pltpu.make_async_copy(wave_hbm, wave_ref, small.at[0]),
        pltpu.make_async_copy(slot_hbm, slot_ref, small.at[1]),
        pltpu.make_async_copy(start_hbm, start_ref, small.at[2]),
        pltpu.make_async_copy(spec_hbm, masked_ref, small.at[3]),
    ]
    for copy in inputs:
        copy.start()
    copies = [
        pltpu.make_async_copy(
            leg_hbm.at[pl.ds(c * CHUNK, CHUNK)], legv_ref.at[pl.ds(c * CHUNK, CHUNK)], sems.at[c]
        )
        for c in range(CHUNKS)
    ]
    for copy in copies:
        copy.start()
    for copy in inputs:
        copy.wait()
    lane = iota((8, 128), 1)
    sub = iota((8, 128), 0)
    offset = row_offset(lane)
    left = lane < 64
    upper = sub < 4
    sign = jnp.where(lane % ROWS < ROWS // 2, 1.0, -1.0).astype(F32)

    waves = [wave_ref[s] for s in range(8)]
    keys = [jnp.where(w % 2 == 1, 2 * NTRUNC - 1 - w, w) for w in waves]
    places = []
    for s in range(8):
        place = jnp.int32(0)
        for other in range(8):
            if other != s:
                place = place + (keys[other] < keys[s]).astype(jnp.int32)
        place_ref[s] = place
        places.append(place)
    ids = jnp.zeros((8, 128), jnp.int32)
    for s in range(8):
        ids = jnp.where(lane // 32 == places[s], waves[s], ids)
    ids = jnp.where(sub == 0, ids >> 4, ids & 15).astype(F32)

    def index(k, carry):
        slot = slot_ref[k]
        pos_ref[k] = place_ref[slot]
        base_ref[k] = wave_ref[slot] + start_ref[k]
        return carry

    lax.fori_loop(0, BLOCKS, index, 0, unroll=12)
    results = [
        pltpu.make_async_copy(pos_ref, pos_hbm, small.at[4]),
        pltpu.make_async_copy(base_ref, base_hbm, small.at[5]),
    ]
    for copy in results:
        copy.start()

    def build(j, carry):
        k0 = 2 * j
        degree = jnp.where(upper, base_ref[k0], base_ref[k0 + 1]) + offset
        here = pl.ds(pl.multiple_of(8 * j, 8), 8)
        own = jnp.where(degree < NTRUNC, masked_ref[here, :], 0.0)
        masked_ref[here, :] = own
        turned = pltpu.roll(own, 64, 1)
        parts = (
            jnp.where(left, own, pltpu.roll(turned, 4, 0)),
            jnp.where(left, turned, pltpu.roll(own, 4, 0)),
        )
        match = jnp.where(left, pos_ref[k0], pos_ref[k0 + 1]) == sub
        for l in range(LEVELS):
            north = jnp.concatenate(
                [
                    jnp.where(match, jnp.broadcast_to(p[l : l + 1], (8, 128)), 0.0)
                    for p in parts
                ],
                axis=0,
            )
            south = north * jnp.concatenate([sign, sign], axis=0)
            lhs_ref[j, 32 * l : 32 * l + 16, :] = north.astype(BF16)
            lhs_ref[j, 32 * l + 16 : 32 * l + 32, :] = south.astype(BF16)
        return carry

    lax.fori_loop(0, BLOCKS // 2, build, 0, unroll=6)

    half = CHUNK // 2
    for c in range(CHUNKS):
        copies[c].wait()
        lhs = jnp.concatenate([lhs_ref[c * half + i] for i in range(half)], axis=1)
        for n in range(LATS // 256):
            rhs = legv_ref[c * CHUNK : (c + 1) * CHUNK, :, 256 * n : 256 * n + 256]
            part = jnp.dot(lhs, rhs.reshape(CHUNK * ROWS, 256), preferred_element_type=F32)
            for i in range(2):
                b = 2 * n + i
                piece = part[:, 128 * i : 128 * i + 128]
                if c > 0:
                    piece = piece + acc_ref[b]
                if c + 1 < CHUNKS:
                    acc_ref[b] = piece
                else:
                    for g in range(8):
                        row = SENT_ROWS * (8 * g + b)
                        send_ref[row : row + 16, :] = piece[16 * g : 16 * g + 16]
                        send_ref[row + 16 : row + 18, :] = ids[0:2]
    out_ref[...] = send_ref[...].astype(BF16)
    for copy in results:
        copy.wait()


def prepare_kernel(
    lev_ref, base_ref, level_ref, depth_ref, mode_ref,
    gain_ref, kron_ref, coef_ref, growth_ref,
):
    lev = lev_ref[0]
    row_pick = (iota((128, ALL_LEVELS), 0) // 8 == iota((128, ALL_LEVELS), 1)).astype(F32)
    col = iota((ALL_LEVELS, 128), 1) // 8
    source_level = ((lev - col // LEVELS) & 3) * LEVELS + col % LEVELS
    col_pick = (iota((ALL_LEVELS, 128), 0) == source_level).astype(F32)
    high = lax.Precision.HIGHEST
    wide = jnp.dot(jnp.dot(row_pick, mode_ref[...], precision=high), col_pick, precision=high)
    wide = jnp.where(iota((128, 128), 0) % 8 == iota((128, 128), 1) % 8, wide, 0.0)
    wide_high = wide.astype(BF16)
    kron_ref[0] = wide_high
    kron_ref[1] = (wide - wide_high.astype(F32)).astype(BF16)

    growth_ref[...] = jnp.zeros_like(growth_ref)
    one = row_offset(iota((1, 128), 1))

    def grow(k, carry):
        degree = (base_ref[k] + one).astype(F32)
        growth_ref[pl.ds(k, 1), :] = degree * (degree + 1.0) / (NTRUNC * NTRUNC)
        return carry

    lax.fori_loop(0, BLOCKS, grow, 0, unroll=12)
    for a in range(ALL_LEVELS):
        gain_ref[a] = 1.0 / (1.0 + depth_ref[a] * growth_ref[...])
        for l in range(LEVELS):
            coef_ref[16 * l + a : 16 * l + a + 1, :] = jnp.full(
                (1, 128), level_ref[lev * LEVELS + l, a], F32
            )


def grid_kernel(in_ref, out_ref, recv_ref, tw_ref, g_ref, send_ref):
    recv_ref[...] = in_ref[...].astype(F32)

    def rows_of(j):
        return recv_ref[pl.ds(j, SOURCES, stride=SENT_ROWS), :]

    lane = iota((32, 128), 1)
    lane8 = iota((8, 128), 1)
    shift = [sincos(((NTRUNC - 1) * (128 * a + lane8)) & (NLON - 1)) for a in range(XTILES)]
    ids = rows_of(16) * 16.0 + rows_of(17)

    for p in range(4):
        whole = jnp.broadcast_to(ids[:, 32 * p : 32 * p + 1], (SOURCES, 128)).astype(jnp.int32)
        for half in range(2):
            wave = whole[32 * half : 32 * half + 32]
            rows = slice(64 * p + 32 * half, 64 * p + 32 * half + 32)
            cos, sin = sincos((wave * lane) & (NLON - 1))
            step_cos, step_sin = sincos((wave * 128) & (NLON - 1))
            for a in range(XTILES):
                c1 = jnp.concatenate([shift[a][0]] * 4, axis=0)
                s1 = jnp.concatenate([shift[a][1]] * 4, axis=0)
                tw_ref[0, a, rows, :] = cos.astype(BF16)
                tw_ref[1, a, rows, :] = sin.astype(BF16)
                tw_ref[2, a, rows, :] = (c1 * cos + s1 * sin).astype(BF16)
                tw_ref[3, a, rows, :] = (s1 * cos - c1 * sin).astype(BF16)
                if a + 1 < XTILES:
                    cos, sin = cos * step_cos - sin * step_sin, sin * step_cos + cos * step_sin

    first_row = (0, 8, 4, 12)
    spectra = [
        jnp.concatenate([rows_of(f + p) for p in range(4)], axis=0).T.astype(BF16)
        for f in first_row
    ]
    for a in range(XTILES):
        ce, se, co, so = [
            jnp.dot(spectra[i], tw_ref[i, a], preferred_element_type=F32) for i in range(4)
        ]
        minus, plus = ce - se, ce + se
        odd_minus, odd_plus = co - so, co + so
        f1, f2, f3, f4 = [
            v * jnp.abs(v)
            for v in (minus + odd_minus, minus - odd_minus, plus + odd_plus, plus - odd_plus)
        ]
        s12, d12, s34, d34 = f1 + f2, f1 - f2, f3 + f4, f3 - f4
        folded = (s12 + s34, s12 - s34, d12 + d34, d12 - d34)
        if a == 0:
            share = jnp.where(iota((1, 128), 1) == 0, 0.5, 1.0)
        else:
            share = jnp.where(iota((1, 128), 1) == 0, 0.5, 0.0)
        for i in range(4):
            value = folded[i]
            if a in (0, XTILES - 1):
                value = value * share
            g_ref[i, a] = value.astype(BF16)
    scale = 1.0 / (512.0 * 64.0)
    for i in range(4):
        total = lax.dot_general(
            jnp.concatenate([tw_ref[i, a] for a in range(XTILES)], axis=1),
            jnp.concatenate([g_ref[i, a] for a in range(XTILES)], axis=1),
            (((1,), (1,)), ((), ())),
            preferred_element_type=F32,
        )
        total = total * (scale if i % 2 == 0 else -scale)
        for p in range(4):
            send_ref[pl.ds(first_row[i] + p, SOURCES, stride=16), :] = total[64 * p : 64 * p + 64]
    out_ref[...] = send_ref[...].reshape(SOURCES, 16, 128).astype(BF16)


def direct_kernel(
    pos_hbm, base_hbm, arrived_ref, weight_ref, drag_ref, masked_ref, legv_ref,
    out_ref, pos_ref, base_ref, v_ref, acc_ref, comb_ref, small,
):
    inputs = [
        pltpu.make_async_copy(pos_hbm, pos_ref, small.at[0]),
        pltpu.make_async_copy(base_hbm, base_ref, small.at[1]),
    ]
    for copy in inputs:
        copy.start()
    for b in range(8):
        cols = slice(128 * b, 128 * b + 128)
        weight = -weight_ref[0:1, cols]
        sides = []
        for l in range(LEVELS):
            north = (weight * drag_ref[l, 0:1, cols]) * arrived_ref[16 * l + b].astype(F32)
            south = (weight * drag_ref[l, 1:2, cols]) * arrived_ref[16 * l + 8 + b].astype(F32)
            sides.append((north + south, north - south))
        for a in range(2):
            for c in range(2):
                for pair in range(2):
                    piece = jnp.concatenate(
                        [sides[2 * pair + i][a][8 * c : 8 * c + 8] for i in range(2)], axis=0
                    )
                    row = (a * 2 + c) * 32 + pair * 16
                    v_ref[b, row : row + 16, :] = piece.astype(BF16)
    comb_ref[...] = jnp.zeros_like(comb_ref)
    lane = iota((8, 128), 1)
    offset = row_offset(iota((4, 128), 1))
    left = lane < 64
    even_rows = lane % ROWS < ROWS // 2
    for copy in inputs:
        copy.wait()

    def finish(group, part, product):
        acc_ref[part, 0:128, :] = product[:, 0:128]
        acc_ref[part, 128:256, :] = product[:, 128:256]
        for q in range(4):
            k = 4 * group + q
            rows = acc_ref[part, pl.ds(128 * (q // 2) + pos_ref[k], 16, stride=8), :]
            value = jnp.where(even_rows, rows[0:8], rows[8:16])
            if q % 2 == 0:
                value = jnp.where(left, value, pltpu.roll(pltpu.roll(value, 64, 1), 4, 0))
            else:
                value = jnp.where(left, pltpu.roll(value, 64, 1), pltpu.roll(value, 4, 0))
            live = base_ref[k] + offset < NTRUNC
            total = jnp.where(live, value[0:4] + masked_ref[pl.ds(4 * k, 4), :], 0.0)
            comb_ref[pl.ds(k, 4, stride=KPAD), :] = total

    def groups_of(step, carry):
        lhs = jnp.concatenate([v_ref[b] for b in range(8)], axis=1)
        for part in range(3):
            group = 3 * step + part
            rhs = legv_ref[pl.ds(4 * group, 4)].reshape(4 * ROWS, LATS)
            product = lax.dot_general(
                lhs, rhs, (((1,), (1,)), ((), ())), preferred_element_type=F32
            )
            finish(group, part, product)
        return carry

    lax.fori_loop(0, BLOCKS // 12, groups_of, 0)
    out_ref[...] = comb_ref[...].astype(BF16)


def vertical_kernel(
    own_ref, one_ref, two_ref, three_ref, gain_ref, kron_ref, coef_ref,
    out_hbm, out_ref, sems,
):
    sources = (own_ref, one_ref, two_ref, three_ref)
    both = jnp.concatenate([kron_ref[0], kron_ref[1]], axis=1)
    copies = []
    for t in range(KPAD // 8):
        stacked = jnp.concatenate(
            [
                s[KPAD * j + 8 * t : KPAD * j + 8 * t + 8, :]
                for s in sources
                for j in range(LEVELS)
            ],
            axis=0,
        )
        modal = jnp.dot(
            both, jnp.concatenate([stacked, stacked], axis=0), preferred_element_type=F32
        )
        results = [None] * LEVELS
        for a in range(ALL_LEVELS):
            scaled = modal[8 * a : 8 * a + 8] * gain_ref[a, 8 * t : 8 * t + 8, :]
            for l in range(LEVELS):
                term = coef_ref[16 * l + a : 16 * l + a + 1, :] * scaled
                results[l] = term if a == 0 else results[l] + term
        count = min(8, BLOCKS - 8 * t)
        for l in range(LEVELS):
            out_ref[pl.ds(32 * t + l, count, stride=LEVELS), :] = results[l][0:count]
        rows = pl.ds(32 * t, 4 * count)
        copies.append(pltpu.make_async_copy(out_ref.at[rows], out_hbm.at[rows], sems.at[t]))
        copies[-1].start()
    for copy in copies:
        copy.wait()


def specs(*kinds):
    spaces = {"s": pltpu.SMEM, "v": pltpu.VMEM, "h": pltpu.HBM, "a": pl.ANY}
    return [pl.BlockSpec(memory_space=spaces[k]) for k in kinds]


def in_hbm(x):
    return pltpu.with_memory_space_constraint(x, pltpu.HBM)


def on_device(
    spectral, legendre, wave_ids, block_slot, block_start, lat_weights, drag, mode_inverse,
    level_modes, depths,
):
    lev = lax.axis_index("lev").astype(jnp.int32).reshape(1)
    spec = spectral.reshape(BLOCKS * LEVELS, 128)
    outgoing, legv, masked, pos, base = pl.pallas_call(
        forward_kernel,
        in_specs=specs("h", "h", "h", "h", "h"),
        out_specs=specs("v", "v", "v", "h", "h"),
        out_shape=(
            jax.ShapeDtypeStruct((SOURCES * SENT_ROWS, 128), BF16),
            pltpu.VMEM((BLOCKS, ROWS, LATS), BF16),
            pltpu.VMEM((BLOCKS * LEVELS, 128), F32),
            jax.ShapeDtypeStruct((BLOCKS,), jnp.int32),
            jax.ShapeDtypeStruct((BLOCKS,), jnp.int32),
        ),
        scratch_shapes=[
            pltpu.SMEM((8,), jnp.int32),
            pltpu.SMEM((BLOCKS,), jnp.int32),
            pltpu.SMEM((BLOCKS,), jnp.int32),
            pltpu.SMEM((8,), jnp.int32),
            pltpu.SMEM((BLOCKS,), jnp.int32),
            pltpu.SMEM((BLOCKS,), jnp.int32),
            pltpu.VMEM((BLOCKS // 2, 128, 128), BF16),
            pltpu.VMEM((8, 128, 128), F32),
            pltpu.VMEM((SOURCES * SENT_ROWS, 128), F32),
            pltpu.SemaphoreType.DMA((CHUNKS,)),
            pltpu.SemaphoreType.DMA((6,)),
        ],
        compiler_params=pltpu.CompilerParams(vmem_limit_bytes=24 * MB),
        name="forward",
    )(*[in_hbm(x) for x in (wave_ids, block_slot, block_start, spec, legendre)])
    pairs = SENT_ROWS // 2
    incoming = lax.all_to_all(
        outgoing.reshape(SOURCES, pairs, 2, 128), "band", split_axis=0, concat_axis=0, tiled=True
    ).reshape(SOURCES * SENT_ROWS, 128)
    filtered = pl.pallas_call(
        grid_kernel,
        in_specs=specs("v"),
        out_specs=specs("v")[0],
        out_shape=jax.ShapeDtypeStruct((SOURCES, 16, 128), BF16),
        scratch_shapes=[
            pltpu.VMEM((SOURCES * SENT_ROWS, 128), F32),
            pltpu.VMEM((4, XTILES, 256, 128), BF16),
            pltpu.VMEM((4, XTILES, 128, 128), BF16),
            pltpu.VMEM((SOURCES * 16, 128), F32),
        ],
        compiler_params=pltpu.CompilerParams(vmem_limit_bytes=16 * MB),
        name="grid",
    )(incoming)
    arrived = lax.all_to_all(filtered, "band", split_axis=0, concat_axis=0, tiled=True)
    combined = pl.pallas_call(
        direct_kernel,
        in_specs=specs("h", "h", "v", "v", "v", "v", "v"),
        out_specs=specs("v")[0],
        out_shape=jax.ShapeDtypeStruct((LEVELS * KPAD, 128), BF16),
        scratch_shapes=[
            pltpu.SMEM((BLOCKS,), jnp.int32),
            pltpu.SMEM((BLOCKS,), jnp.int32),
            pltpu.VMEM((8, 128, 128), BF16),
            pltpu.VMEM((3, 256, 128), F32),
            pltpu.VMEM((LEVELS * KPAD, 128), F32),
            pltpu.SemaphoreType.DMA((2,)),
        ],
        compiler_params=pltpu.CompilerParams(vmem_limit_bytes=16 * MB),
        name="direct",
    )(pos, base, arrived, lat_weights.reshape(1, LATS), drag, masked, legv)
    others = [
        lax.ppermute(combined, "lev", [(i, (i + s) % 4) for i in range(4)]) for s in (1, 2, 3)
    ]
    late_base, combined = lax.optimization_barrier((base, combined))
    gain, kron, coef = pl.pallas_call(
        prepare_kernel,
        in_specs=specs("s", "s", "s", "s", "v"),
        out_specs=specs("v", "v", "v"),
        out_shape=(
            pltpu.VMEM((ALL_LEVELS, KPAD, 128), F32),
            pltpu.VMEM((2, 128, 128), BF16),
            pltpu.VMEM((LEVELS * ALL_LEVELS, 128), F32),
        ),
        scratch_shapes=[pltpu.VMEM((KPAD, 128), F32)],
        compiler_params=pltpu.CompilerParams(vmem_limit_bytes=24 * MB),
        name="prepare",
    )(lev, late_base, level_modes, depths, mode_inverse)
    result = pl.pallas_call(
        vertical_kernel,
        in_specs=specs("v", "v", "v", "v", "v", "v", "v"),
        out_specs=specs("h")[0],
        out_shape=jax.ShapeDtypeStruct((BLOCKS * LEVELS, 128), F32),
        scratch_shapes=[
            pltpu.VMEM((BLOCKS * LEVELS, 128), F32),
            pltpu.SemaphoreType.DMA((KPAD // 8,)),
        ],
        compiler_params=pltpu.CompilerParams(vmem_limit_bytes=16 * MB),
        name="vertical",
    )(combined, *others, gain, kron, coef)
    return result.reshape(BLOCKS, LEVELS, 128)


def solution(mesh):
    placed = (
        P("band", "lev", None),
        P("band", None, None),
        P("band"),
        P("band"),
        P("band"),
        P(),
        P("lev", None, None),
        P(),
        P(),
        P(),
    )
    return jax.shard_map(
        on_device, mesh=mesh, in_specs=placed, out_specs=P("band", "lev", None), check_vma=False
    )
```

```python
import math

import jax
import jax.numpy as jnp
from jax import lax
from jax.experimental import pallas as pl
from jax.experimental.pallas import tpu as pltpu
from jax.sharding import PartitionSpec as P

NTRUNC = 1280
NLON = 4096
BLOCKS = 84
ROWS = 64
LATS = 1024
LEVELS = 4
ALL_LEVELS = 16
SOURCES = 64
SENT_ROWS = 18
CHUNK = 12
CHUNKS = BLOCKS // CHUNK
KPAD = 88
XPAD = 1152
TURNED = 2
AHEAD = 5
XTILES = XPAD // 128
F32 = jnp.float32
BF16 = jnp.bfloat16
MB = 1024 * 1024


def iota(shape, dim):
    return lax.broadcasted_iota(jnp.int32, shape, dim)


def row_offset(lane):
    r = lane % ROWS
    half = ROWS // 2
    return jnp.where(r < half, 2 * r, 2 * (r - half) + 1)


def sincos(turns):
    quarter = ((turns + 512) >> 10) & 3
    rest = ((turns + 512) & 1023) - 512
    t = rest.astype(F32) * (2.0 * math.pi / NLON)
    z = t * t
    s = t * (1.0 + z * (-1.0 / 6 + z * (1.0 / 120 + z * (-1.0 / 5040 + z * (1.0 / 362880)))))
    c = 1.0 + z * (-0.5 + z * (1.0 / 24 + z * (-1.0 / 720 + z * (1.0 / 40320))))
    swap = (quarter & 1) == 1
    cos = jnp.where(swap, s, c)
    sin = jnp.where(swap, c, s)
    cos = jnp.where((quarter == 1) | (quarter == 2), -cos, cos)
    sin = jnp.where(quarter >= 2, -sin, sin)
    return cos, sin


def forward_kernel(
    wave_hbm, slot_hbm, start_hbm, spec_hbm, leg_hbm,
    out_ref, legv_ref, masked_ref, pos_hbm, base_hbm,
    wave_ref, slot_ref, start_ref, place_ref, pos_ref, base_ref, lhs_ref, acc_ref, send_ref,
    sems, small,
):
    inputs = [
        pltpu.make_async_copy(wave_hbm, wave_ref, small.at[0]),
        pltpu.make_async_copy(slot_hbm, slot_ref, small.at[1]),
        pltpu.make_async_copy(start_hbm, start_ref, small.at[2]),
        pltpu.make_async_copy(spec_hbm, masked_ref, small.at[3]),
    ]
    for copy in inputs:
        copy.start()
    copies = [
        pltpu.make_async_copy(
            leg_hbm.at[pl.ds(c * CHUNK, CHUNK)], legv_ref.at[pl.ds(c * CHUNK, CHUNK)], sems.at[c]
        )
        for c in range(CHUNKS)
    ]
    for copy in copies[:AHEAD]:
        copy.start()
    for copy in inputs:
        copy.wait()
    lane = iota((8, 128), 1)
    sub = iota((8, 128), 0)
    offset = row_offset(lane)
    left = lane < 64
    upper = sub < 4
    sign = jnp.where(lane % ROWS < ROWS // 2, 1.0, -1.0).astype(F32)

    waves = [wave_ref[s] for s in range(8)]
    keys = [jnp.where(w % 2 == 1, 2 * NTRUNC - 1 - w, w) for w in waves]
    places = []
    for s in range(8):
        place = jnp.int32(0)
        for other in range(8):
            if other != s:
                place = place + (keys[other] < keys[s]).astype(jnp.int32)
        place_ref[s] = place
        places.append(place)
    ids = jnp.zeros((8, 128), jnp.int32)
    for s in range(8):
        ids = jnp.where(lane // 32 == places[s], waves[s], ids)
    ids = jnp.where(sub == 0, ids >> 4, ids & 15).astype(F32)

    def index(k, carry):
        slot = slot_ref[k]
        pos_ref[k] = place_ref[slot]
        base_ref[k] = wave_ref[slot] + start_ref[k]
        return carry

    lax.fori_loop(0, BLOCKS, index, 0, unroll=12)
    results = [
        pltpu.make_async_copy(pos_ref, pos_hbm, small.at[4]),
        pltpu.make_async_copy(base_ref, base_hbm, small.at[5]),
    ]
    for copy in results:
        copy.start()

    def build(j, carry):
        k0 = 2 * j
        degree = jnp.where(upper, base_ref[k0], base_ref[k0 + 1]) + offset
        here = pl.ds(pl.multiple_of(8 * j, 8), 8)
        own = jnp.where(degree < NTRUNC, masked_ref[here, :], 0.0)
        masked_ref[here, :] = own
        turned = pltpu.roll(own, 64, 1)
        parts = (
            jnp.where(left, own, pltpu.roll(turned, 4, 0)),
            jnp.where(left, turned, pltpu.roll(own, 4, 0)),
        )
        match = jnp.where(left, pos_ref[k0], pos_ref[k0 + 1]) == sub
        for l in range(LEVELS):
            north = jnp.concatenate(
                [
                    jnp.where(match, jnp.broadcast_to(p[l : l + 1], (8, 128)), 0.0)
                    for p in parts
                ],
                axis=0,
            )
            south = north * jnp.concatenate([sign, sign], axis=0)
            lhs_ref[j, 32 * l : 32 * l + 16, :] = north.astype(BF16)
            lhs_ref[j, 32 * l + 16 : 32 * l + 32, :] = south.astype(BF16)
        return carry

    half = CHUNK // 2

    def build_chunk(c):
        lax.fori_loop(c * half, (c + 1) * half, build, 0, unroll=half)

    build_chunk(0)
    for c in range(CHUNKS):
        copies[c].wait()
        if c + AHEAD < CHUNKS:
            copies[c + AHEAD].start()
        if c + 1 < CHUNKS:
            build_chunk(c + 1)
        lhs = jnp.concatenate([lhs_ref[c * half + i] for i in range(half)], axis=1)
        for n in range(LATS // 256):
            rhs = legv_ref[c * CHUNK : (c + 1) * CHUNK, :, 256 * n : 256 * n + 256]
            part = jnp.dot(lhs, rhs.reshape(CHUNK * ROWS, 256), preferred_element_type=F32)
            for i in range(2):
                b = 2 * n + i
                piece = part[:, 128 * i : 128 * i + 128]
                if c > 0:
                    piece = piece + acc_ref[b]
                if c + 1 < CHUNKS:
                    acc_ref[b] = piece
                else:
                    for g in range(8):
                        row = SENT_ROWS * (8 * g + b)
                        send_ref[row : row + 16, :] = piece[16 * g : 16 * g + 16]
                        send_ref[row + 16 : row + 18, :] = ids[0:2]
    out_ref[...] = send_ref[...].astype(BF16)
    for copy in results:
        copy.wait()


def prepare_kernel(
    lev_ref, base_ref, level_ref, depth_ref, mode_ref,
    gain_ref, kron_ref, coef_ref, growth_ref,
):
    lev = lev_ref[0]
    row_pick = (iota((128, ALL_LEVELS), 0) // 8 == iota((128, ALL_LEVELS), 1)).astype(F32)
    col = iota((ALL_LEVELS, 128), 1) // 8
    source_level = ((lev - col // LEVELS) & 3) * LEVELS + col % LEVELS
    col_pick = (iota((ALL_LEVELS, 128), 0) == source_level).astype(F32)
    high = lax.Precision.HIGHEST
    wide = jnp.dot(jnp.dot(row_pick, mode_ref[...], precision=high), col_pick, precision=high)
    wide = jnp.where(iota((128, 128), 0) % 8 == iota((128, 128), 1) % 8, wide, 0.0)
    wide_high = wide.astype(BF16)
    kron_ref[0] = wide_high
    kron_ref[1] = (wide - wide_high.astype(F32)).astype(BF16)

    growth_ref[...] = jnp.zeros_like(growth_ref)
    one = row_offset(iota((1, 128), 1))

    def grow(k, carry):
        degree = (base_ref[k] + one).astype(F32)
        growth_ref[pl.ds(k, 1), :] = degree * (degree + 1.0) / (NTRUNC * NTRUNC)
        return carry

    lax.fori_loop(0, BLOCKS, grow, 0, unroll=12)
    for a in range(ALL_LEVELS):
        gain_ref[a] = 1.0 / (1.0 + depth_ref[a] * growth_ref[...])
        for l in range(LEVELS):
            coef_ref[16 * l + a : 16 * l + a + 1, :] = jnp.full(
                (1, 128), level_ref[lev * LEVELS + l, a], F32
            )


def grid_kernel(in_ref, out_ref, recv_ref, tw_ref, g_ref, send_ref):
    recv_ref[...] = in_ref[...].astype(F32)

    def rows_of(j):
        return recv_ref[pl.ds(j, SOURCES, stride=SENT_ROWS), :]

    lane = iota((32, 128), 1)
    lane8 = iota((8, 128), 1)
    shift = [sincos(((NTRUNC - 1) * (128 * a + lane8)) & (NLON - 1)) for a in range(XTILES)]
    ids = rows_of(16) * 16.0 + rows_of(17)

    for p in range(4):
        whole = jnp.broadcast_to(ids[:, 32 * p : 32 * p + 1], (SOURCES, 128)).astype(jnp.int32)
        for half in range(2):
            wave = whole[32 * half : 32 * half + 32]
            rows = slice(64 * p + 32 * half, 64 * p + 32 * half + 32)
            cos, sin = sincos((wave * lane) & (NLON - 1))
            step_cos, step_sin = sincos((wave * 128) & (NLON - 1))
            for a in range(XTILES):
                c1 = jnp.concatenate([shift[a][0]] * 4, axis=0)
                s1 = jnp.concatenate([shift[a][1]] * 4, axis=0)
                tw_ref[0, a, rows, :] = cos.astype(BF16)
                tw_ref[1, a, rows, :] = sin.astype(BF16)
                tw_ref[2, a, rows, :] = (c1 * cos + s1 * sin).astype(BF16)
                tw_ref[3, a, rows, :] = (s1 * cos - c1 * sin).astype(BF16)
                if a + 1 < XTILES:
                    cos, sin = cos * step_cos - sin * step_sin, sin * step_cos + cos * step_sin

    first_row = (0, 8, 4, 12)
    spectra = [
        jnp.concatenate([rows_of(f + p) for p in range(4)], axis=0).T.astype(BF16)
        for f in first_row
    ]
    for a in range(XTILES):
        ce, se, co, so = [
            jnp.dot(spectra[i], tw_ref[i, a], preferred_element_type=F32) for i in range(4)
        ]
        minus, plus = ce - se, ce + se
        odd_minus, odd_plus = co - so, co + so
        f1, f2, f3, f4 = [
            v * jnp.abs(v)
            for v in (minus + odd_minus, minus - odd_minus, plus + odd_plus, plus - odd_plus)
        ]
        s12, d12, s34, d34 = f1 + f2, f1 - f2, f3 + f4, f3 - f4
        folded = (s12 + s34, s12 - s34, d12 + d34, d12 - d34)
        if a == 0:
            share = jnp.where(iota((1, 128), 1) == 0, 0.5, 1.0)
        else:
            share = jnp.where(iota((1, 128), 1) == 0, 0.5, 0.0)
        for i in range(4):
            value = folded[i]
            if a in (0, XTILES - 1):
                value = value * share
            g_ref[i, a] = value.astype(BF16)
    scale = 1.0 / (512.0 * 64.0)
    for i in range(4):
        total = lax.dot_general(
            jnp.concatenate([tw_ref[i, a] for a in range(XTILES)], axis=1),
            jnp.concatenate([g_ref[i, a] for a in range(XTILES)], axis=1),
            (((1,), (1,)), ((), ())),
            preferred_element_type=F32,
        )
        total = total * (scale if i % 2 == 0 else -scale)
        for p in range(4):
            send_ref[pl.ds(first_row[i] + p, SOURCES, stride=16), :] = total[64 * p : 64 * p + 64]
    out_ref[...] = send_ref[...].reshape(SOURCES, 16, 128).astype(BF16)


def direct_kernel(
    pos_hbm, base_hbm, arrived_ref, weight_ref, drag_ref, masked_ref, legv_ref,
    out_ref, pos_ref, base_ref, v_ref, acc_ref, comb_ref, turned_ref, small,
):
    inputs = [
        pltpu.make_async_copy(pos_hbm, pos_ref, small.at[0]),
        pltpu.make_async_copy(base_hbm, base_ref, small.at[1]),
    ]
    for copy in inputs:
        copy.start()
    for b in range(8):
        cols = slice(128 * b, 128 * b + 128)
        weight = -weight_ref[0:1, cols]
        sides = []
        for l in range(LEVELS):
            north = (weight * drag_ref[l, 0:1, cols]) * arrived_ref[16 * l + b].astype(F32)
            south = (weight * drag_ref[l, 1:2, cols]) * arrived_ref[16 * l + 8 + b].astype(F32)
            sides.append((north + south, north - south))
        for a in range(2):
            for c in range(2):
                for pair in range(2):
                    piece = jnp.concatenate(
                        [sides[2 * pair + i][a][8 * c : 8 * c + 8] for i in range(2)], axis=0
                    )
                    row = (a * 2 + c) * 32 + pair * 16
                    v_ref[b, row : row + 16, :] = piece.astype(BF16)
    comb_ref[...] = jnp.zeros_like(comb_ref)
    lane = iota((8, 128), 1)
    offset = row_offset(iota((4, 128), 1))
    left = lane < 64
    even_rows = lane % ROWS < ROWS // 2
    for copy in inputs:
        copy.wait()

    def finish(group, part, product):
        acc_ref[part, 0:128, :] = product[:, 0:128]
        acc_ref[part, 128:256, :] = product[:, 128:256]
        for q in range(4):
            k = 4 * group + q
            rows = acc_ref[part, pl.ds(128 * (q // 2) + pos_ref[k], 16, stride=8), :]
            value = jnp.where(even_rows, rows[0:8], rows[8:16])
            if q % 2 == 0:
                value = jnp.where(left, value, pltpu.roll(pltpu.roll(value, 64, 1), 4, 0))
            else:
                value = jnp.where(left, pltpu.roll(value, 64, 1), pltpu.roll(value, 4, 0))
            live = base_ref[k] + offset < NTRUNC
            total = jnp.where(live, value[0:4] + masked_ref[pl.ds(4 * k, 4), :], 0.0)
            comb_ref[pl.ds(k, 4, stride=KPAD), :] = total

    steps = BLOCKS // 12

    def turn(step):
        for part in range(TURNED):
            group = 3 * step + part
            for i in range(2):
                for b in range(8):
                    tile = legv_ref[
                        4 * group + 2 * i : 4 * group + 2 * i + 2, :, 128 * b : 128 * b + 128
                    ]
                    turned_ref[2 * (step % 2) + part, i, 128 * b : 128 * b + 128, :] = (
                        tile.reshape(128, 128).T
                    )

    turn(0)
    for step in range(steps):
        lhs = jnp.concatenate([v_ref[b] for b in range(8)], axis=1)
        if step + 1 < steps:
            turn(step + 1)
        for part in (2, 0, 1):
            group = 3 * step + part
            if part < TURNED:
                slot = 2 * (step % 2) + part
                rhs = jnp.concatenate([turned_ref[slot, 0], turned_ref[slot, 1]], axis=1)
                product = jnp.dot(lhs, rhs, preferred_element_type=F32)
            else:
                rhs = legv_ref[4 * group : 4 * group + 4].reshape(4 * ROWS, LATS)
                product = lax.dot_general(
                    lhs, rhs, (((1,), (1,)), ((), ())), preferred_element_type=F32
                )
            finish(group, part + 3 * (step % 2), product)
    out_ref[...] = comb_ref[...].astype(BF16)


def vertical_kernel(
    own_ref, one_ref, two_ref, three_ref, gain_ref, kron_ref, coef_ref,
    out_hbm, out_ref, sems,
):
    sources = (own_ref, one_ref, two_ref, three_ref)
    both = jnp.concatenate([kron_ref[0], kron_ref[1]], axis=1)
    copies = []
    for t in range(KPAD // 8):
        stacked = jnp.concatenate(
            [
                s[KPAD * j + 8 * t : KPAD * j + 8 * t + 8, :]
                for s in sources
                for j in range(LEVELS)
            ],
            axis=0,
        )
        modal = jnp.dot(
            both, jnp.concatenate([stacked, stacked], axis=0), preferred_element_type=F32
        )
        results = [None] * LEVELS
        for a in range(ALL_LEVELS):
            scaled = modal[8 * a : 8 * a + 8] * gain_ref[a, 8 * t : 8 * t + 8, :]
            for l in range(LEVELS):
                term = coef_ref[16 * l + a : 16 * l + a + 1, :] * scaled
                results[l] = term if a == 0 else results[l] + term
        count = min(8, BLOCKS - 8 * t)
        for l in range(LEVELS):
            out_ref[pl.ds(32 * t + l, count, stride=LEVELS), :] = results[l][0:count]
        rows = pl.ds(32 * t, 4 * count)
        copies.append(pltpu.make_async_copy(out_ref.at[rows], out_hbm.at[rows], sems.at[t]))
        copies[-1].start()
    for copy in copies:
        copy.wait()


def specs(*kinds):
    spaces = {"s": pltpu.SMEM, "v": pltpu.VMEM, "h": pltpu.HBM, "a": pl.ANY}
    return [pl.BlockSpec(memory_space=spaces[k]) for k in kinds]


def in_hbm(x):
    return pltpu.with_memory_space_constraint(x, pltpu.HBM)


def on_device(
    spectral, legendre, wave_ids, block_slot, block_start, lat_weights, drag, mode_inverse,
    level_modes, depths,
):
    lev = lax.axis_index("lev").astype(jnp.int32).reshape(1)
    spec = spectral.reshape(BLOCKS * LEVELS, 128)
    outgoing, legv, masked, pos, base = pl.pallas_call(
        forward_kernel,
        in_specs=specs("h", "h", "h", "h", "h"),
        out_specs=specs("v", "v", "v", "h", "h"),
        out_shape=(
            jax.ShapeDtypeStruct((SOURCES * SENT_ROWS, 128), BF16),
            pltpu.VMEM((BLOCKS, ROWS, LATS), BF16),
            pltpu.VMEM((BLOCKS * LEVELS, 128), F32),
            jax.ShapeDtypeStruct((BLOCKS,), jnp.int32),
            jax.ShapeDtypeStruct((BLOCKS,), jnp.int32),
        ),
        scratch_shapes=[
            pltpu.SMEM((8,), jnp.int32),
            pltpu.SMEM((BLOCKS,), jnp.int32),
            pltpu.SMEM((BLOCKS,), jnp.int32),
            pltpu.SMEM((8,), jnp.int32),
            pltpu.SMEM((BLOCKS,), jnp.int32),
            pltpu.SMEM((BLOCKS,), jnp.int32),
            pltpu.VMEM((BLOCKS // 2, 128, 128), BF16),
            pltpu.VMEM((8, 128, 128), F32),
            pltpu.VMEM((SOURCES * SENT_ROWS, 128), F32),
            pltpu.SemaphoreType.DMA((CHUNKS,)),
            pltpu.SemaphoreType.DMA((6,)),
        ],
        compiler_params=pltpu.CompilerParams(vmem_limit_bytes=24 * MB),
        name="forward",
    )(*[in_hbm(x) for x in (wave_ids, block_slot, block_start, spec, legendre)])
    pairs = SENT_ROWS // 2
    incoming = lax.all_to_all(
        outgoing.reshape(SOURCES, pairs, 2, 128), "band", split_axis=0, concat_axis=0, tiled=True
    ).reshape(SOURCES * SENT_ROWS, 128)
    filtered = pl.pallas_call(
        grid_kernel,
        in_specs=specs("v"),
        out_specs=specs("v")[0],
        out_shape=jax.ShapeDtypeStruct((SOURCES, 16, 128), BF16),
        scratch_shapes=[
            pltpu.VMEM((SOURCES * SENT_ROWS, 128), F32),
            pltpu.VMEM((4, XTILES, 256, 128), BF16),
            pltpu.VMEM((4, XTILES, 128, 128), BF16),
            pltpu.VMEM((SOURCES * 16, 128), F32),
        ],
        compiler_params=pltpu.CompilerParams(vmem_limit_bytes=16 * MB),
        name="grid",
    )(incoming)
    arrived = lax.all_to_all(filtered, "band", split_axis=0, concat_axis=0, tiled=True)
    combined = pl.pallas_call(
        direct_kernel,
        in_specs=specs("h", "h", "v", "v", "v", "v", "v"),
        out_specs=specs("v")[0],
        out_shape=jax.ShapeDtypeStruct((LEVELS * KPAD, 128), BF16),
        scratch_shapes=[
            pltpu.SMEM((BLOCKS,), jnp.int32),
            pltpu.SMEM((BLOCKS,), jnp.int32),
            pltpu.VMEM((8, 128, 128), BF16),
            pltpu.VMEM((6, 256, 128), F32),
            pltpu.VMEM((LEVELS * KPAD, 128), F32),
            pltpu.VMEM((4, 2, LATS, 128), BF16),
            pltpu.SemaphoreType.DMA((2,)),
        ],
        compiler_params=pltpu.CompilerParams(vmem_limit_bytes=16 * MB),
        name="direct",
    )(pos, base, arrived, lat_weights.reshape(1, LATS), drag, masked, legv)
    others = [
        lax.ppermute(combined, "lev", [(i, (i + s) % 4) for i in range(4)]) for s in (1, 2, 3)
    ]
    late_base, combined = lax.optimization_barrier((base, combined))
    gain, kron, coef = pl.pallas_call(
        prepare_kernel,
        in_specs=specs("s", "s", "s", "s", "v"),
        out_specs=specs("v", "v", "v"),
        out_shape=(
            pltpu.VMEM((ALL_LEVELS, KPAD, 128), F32),
            pltpu.VMEM((2, 128, 128), BF16),
            pltpu.VMEM((LEVELS * ALL_LEVELS, 128), F32),
        ),
        scratch_shapes=[pltpu.VMEM((KPAD, 128), F32)],
        compiler_params=pltpu.CompilerParams(vmem_limit_bytes=24 * MB),
        name="prepare",
    )(lev, late_base, level_modes, depths, mode_inverse)
    result = pl.pallas_call(
        vertical_kernel,
        in_specs=specs("v", "v", "v", "v", "v", "v", "v"),
        out_specs=specs("h")[0],
        out_shape=jax.ShapeDtypeStruct((BLOCKS * LEVELS, 128), F32),
        scratch_shapes=[
            pltpu.VMEM((BLOCKS * LEVELS, 128), F32),
            pltpu.SemaphoreType.DMA((KPAD // 8,)),
        ],
        compiler_params=pltpu.CompilerParams(vmem_limit_bytes=16 * MB),
        name="vertical",
    )(combined, *others, gain, kron, coef)
    return result.reshape(BLOCKS, LEVELS, 128)


def solution(mesh):
    placed = (
        P("band", "lev", None),
        P("band", None, None),
        P("band"),
        P("band"),
        P("band"),
        P(),
        P("lev", None, None),
        P(),
        P(),
        P(),
    )
    return jax.shard_map(
        on_device, mesh=mesh, in_specs=placed, out_specs=P("band", "lev", None), check_vma=False
    )
```

```python
import math

import jax
import jax.numpy as jnp
from jax import lax
from jax.experimental import pallas as pl
from jax.experimental.pallas import tpu as pltpu
from jax.sharding import PartitionSpec as P

NTRUNC = 1280
NLON = 4096
BLOCKS = 84
ROWS = 64
LATS = 1024
LEVELS = 4
ALL_LEVELS = 16
SOURCES = 64
SENT_ROWS = 18
CHUNK = 12
CHUNKS = BLOCKS // CHUNK
KPAD = 88
XPAD = 1152
TURNED = 2
AHEAD = 5
XTILES = XPAD // 128
F32 = jnp.float32
BF16 = jnp.bfloat16
MB = 1024 * 1024


def iota(shape, dim):
    return lax.broadcasted_iota(jnp.int32, shape, dim)


def row_offset(lane):
    r = lane % ROWS
    half = ROWS // 2
    return jnp.where(r < half, 2 * r, 2 * (r - half) + 1)


def sincos(turns):
    quarter = ((turns + 512) >> 10) & 3
    rest = ((turns + 512) & 1023) - 512
    t = rest.astype(F32) * (2.0 * math.pi / NLON)
    z = t * t
    s = t * (1.0 + z * (-1.0 / 6 + z * (1.0 / 120 + z * (-1.0 / 5040 + z * (1.0 / 362880)))))
    c = 1.0 + z * (-0.5 + z * (1.0 / 24 + z * (-1.0 / 720 + z * (1.0 / 40320))))
    swap = (quarter & 1) == 1
    cos = jnp.where(swap, s, c)
    sin = jnp.where(swap, c, s)
    cos = jnp.where((quarter == 1) | (quarter == 2), -cos, cos)
    sin = jnp.where(quarter >= 2, -sin, sin)
    return cos, sin


def forward_kernel(
    wave_hbm, slot_hbm, start_hbm, spec_hbm, leg_hbm,
    out_ref, legv_ref, masked_ref, pos_hbm, base_hbm,
    wave_ref, slot_ref, start_ref, place_ref, pos_ref, base_ref, lhs_ref, acc_ref, send_ref,
    sems, small,
):
    inputs = [
        pltpu.make_async_copy(wave_hbm, wave_ref, small.at[0]),
        pltpu.make_async_copy(slot_hbm, slot_ref, small.at[1]),
        pltpu.make_async_copy(start_hbm, start_ref, small.at[2]),
        pltpu.make_async_copy(spec_hbm, masked_ref, small.at[3]),
    ]
    for copy in inputs:
        copy.start()
    copies = [
        pltpu.make_async_copy(
            leg_hbm.at[pl.ds(c * CHUNK, CHUNK)], legv_ref.at[pl.ds(c * CHUNK, CHUNK)], sems.at[c]
        )
        for c in range(CHUNKS)
    ]
    for c in range(AHEAD):
        copies[c].start(priority=c % 2)
    for copy in inputs:
        copy.wait()
    lane = iota((8, 128), 1)
    sub = iota((8, 128), 0)
    offset = row_offset(lane)
    left = lane < 64
    upper = sub < 4
    sign = jnp.where(lane % ROWS < ROWS // 2, 1.0, -1.0).astype(F32)

    waves = [wave_ref[s] for s in range(8)]
    keys = [jnp.where(w % 2 == 1, 2 * NTRUNC - 1 - w, w) for w in waves]
    places = []
    for s in range(8):
        place = jnp.int32(0)
        for other in range(8):
            if other != s:
                place = place + (keys[other] < keys[s]).astype(jnp.int32)
        place_ref[s] = place
        places.append(place)
    ids = jnp.zeros((8, 128), jnp.int32)
    for s in range(8):
        ids = jnp.where(lane // 32 == places[s], waves[s], ids)
    ids = jnp.where(sub == 0, ids >> 4, ids & 15).astype(F32)

    def index(k, carry):
        slot = slot_ref[k]
        pos_ref[k] = place_ref[slot]
        base_ref[k] = wave_ref[slot] + start_ref[k]
        return carry

    lax.fori_loop(0, BLOCKS, index, 0, unroll=12)
    results = [
        pltpu.make_async_copy(pos_ref, pos_hbm, small.at[4]),
        pltpu.make_async_copy(base_ref, base_hbm, small.at[5]),
    ]
    for copy in results:
        copy.start()

    def build(j, carry):
        k0 = 2 * j
        degree = jnp.where(upper, base_ref[k0], base_ref[k0 + 1]) + offset
        here = pl.ds(pl.multiple_of(8 * j, 8), 8)
        own = jnp.where(degree < NTRUNC, masked_ref[here, :], 0.0)
        masked_ref[here, :] = own
        turned = pltpu.roll(own, 64, 1)
        parts = (
            jnp.where(left, own, pltpu.roll(turned, 4, 0)),
            jnp.where(left, turned, pltpu.roll(own, 4, 0)),
        )
        match = jnp.where(left, pos_ref[k0], pos_ref[k0 + 1]) == sub
        for l in range(LEVELS):
            north = jnp.concatenate(
                [
                    jnp.where(match, jnp.broadcast_to(p[l : l + 1], (8, 128)), 0.0)
                    for p in parts
                ],
                axis=0,
            )
            south = north * jnp.concatenate([sign, sign], axis=0)
            lhs_ref[j, 32 * l : 32 * l + 16, :] = north.astype(BF16)
            lhs_ref[j, 32 * l + 16 : 32 * l + 32, :] = south.astype(BF16)
        return carry

    half = CHUNK // 2

    def build_chunk(c):
        lax.fori_loop(c * half, (c + 1) * half, build, 0, unroll=half)

    build_chunk(0)
    for c in range(CHUNKS):
        copies[c].wait()
        if c + AHEAD < CHUNKS:
            copies[c + AHEAD].start(priority=(c + AHEAD) % 2)
        if c + 1 < CHUNKS:
            build_chunk(c + 1)
        lhs = jnp.concatenate([lhs_ref[c * half + i] for i in range(half)], axis=1)
        for n in range(LATS // 256):
            rhs = legv_ref[c * CHUNK : (c + 1) * CHUNK, :, 256 * n : 256 * n + 256]
            part = jnp.dot(lhs, rhs.reshape(CHUNK * ROWS, 256), preferred_element_type=F32)
            for i in range(2):
                b = 2 * n + i
                piece = part[:, 128 * i : 128 * i + 128]
                if c > 0:
                    piece = piece + acc_ref[b]
                if c + 1 < CHUNKS:
                    acc_ref[b] = piece
                else:
                    for g in range(8):
                        row = SENT_ROWS * (8 * g + b)
                        send_ref[row : row + 16, :] = piece[16 * g : 16 * g + 16]
                        send_ref[row + 16 : row + 18, :] = ids[0:2]
    out_ref[...] = send_ref[...].astype(BF16)
    for copy in results:
        copy.wait()


def prepare_kernel(
    lev_ref, base_ref, level_ref, depth_ref, mode_ref,
    gain_ref, kron_ref, coef_ref, growth_ref,
):
    lev = lev_ref[0]
    row_pick = (iota((128, ALL_LEVELS), 0) // 8 == iota((128, ALL_LEVELS), 1)).astype(F32)
    col = iota((ALL_LEVELS, 128), 1) // 8
    source_level = ((lev - col // LEVELS) & 3) * LEVELS + col % LEVELS
    col_pick = (iota((ALL_LEVELS, 128), 0) == source_level).astype(F32)
    high = lax.Precision.HIGHEST
    wide = jnp.dot(jnp.dot(row_pick, mode_ref[...], precision=high), col_pick, precision=high)
    wide = jnp.where(iota((128, 128), 0) % 8 == iota((128, 128), 1) % 8, wide, 0.0)
    wide_high = wide.astype(BF16)
    kron_ref[0] = wide_high
    kron_ref[1] = (wide - wide_high.astype(F32)).astype(BF16)

    growth_ref[...] = jnp.zeros_like(growth_ref)
    one = row_offset(iota((1, 128), 1))

    def grow(k, carry):
        degree = (base_ref[k] + one).astype(F32)
        growth_ref[pl.ds(k, 1), :] = degree * (degree + 1.0) / (NTRUNC * NTRUNC)
        return carry

    lax.fori_loop(0, BLOCKS, grow, 0, unroll=12)
    for a in range(ALL_LEVELS):
        gain_ref[a] = 1.0 / (1.0 + depth_ref[a] * growth_ref[...])
        for l in range(LEVELS):
            coef_ref[16 * l + a : 16 * l + a + 1, :] = jnp.full(
                (1, 128), level_ref[lev * LEVELS + l, a], F32
            )


def grid_kernel(in_ref, out_ref, recv_ref, tw_ref, g_ref, send_ref):
    recv_ref[...] = in_ref[...].astype(F32)

    def rows_of(j):
        return recv_ref[pl.ds(j, SOURCES, stride=SENT_ROWS), :]

    lane = iota((32, 128), 1)
    lane8 = iota((8, 128), 1)
    shift = [sincos(((NTRUNC - 1) * (128 * a + lane8)) & (NLON - 1)) for a in range(XTILES)]
    ids = rows_of(16) * 16.0 + rows_of(17)

    for p in range(4):
        whole = jnp.broadcast_to(ids[:, 32 * p : 32 * p + 1], (SOURCES, 128)).astype(jnp.int32)
        for half in range(2):
            wave = whole[32 * half : 32 * half + 32]
            rows = slice(64 * p + 32 * half, 64 * p + 32 * half + 32)
            cos, sin = sincos((wave * lane) & (NLON - 1))
            step_cos, step_sin = sincos((wave * 128) & (NLON - 1))
            for a in range(XTILES):
                c1 = jnp.concatenate([shift[a][0]] * 4, axis=0)
                s1 = jnp.concatenate([shift[a][1]] * 4, axis=0)
                tw_ref[0, a, rows, :] = cos.astype(BF16)
                tw_ref[1, a, rows, :] = sin.astype(BF16)
                tw_ref[2, a, rows, :] = (c1 * cos + s1 * sin).astype(BF16)
                tw_ref[3, a, rows, :] = (s1 * cos - c1 * sin).astype(BF16)
                if a + 1 < XTILES:
                    cos, sin = cos * step_cos - sin * step_sin, sin * step_cos + cos * step_sin

    first_row = (0, 8, 4, 12)
    spectra = [
        jnp.concatenate([rows_of(f + p) for p in range(4)], axis=0).T.astype(BF16)
        for f in first_row
    ]
    for a in range(XTILES):
        ce, se, co, so = [
            jnp.dot(spectra[i], tw_ref[i, a], preferred_element_type=F32) for i in range(4)
        ]
        minus, plus = ce - se, ce + se
        odd_minus, odd_plus = co - so, co + so
        f1, f2, f3, f4 = [
            v * jnp.abs(v)
            for v in (minus + odd_minus, minus - odd_minus, plus + odd_plus, plus - odd_plus)
        ]
        s12, d12, s34, d34 = f1 + f2, f1 - f2, f3 + f4, f3 - f4
        folded = (s12 + s34, s12 - s34, d12 + d34, d12 - d34)
        if a == 0:
            share = jnp.where(iota((1, 128), 1) == 0, 0.5, 1.0)
        else:
            share = jnp.where(iota((1, 128), 1) == 0, 0.5, 0.0)
        for i in range(4):
            value = folded[i]
            if a in (0, XTILES - 1):
                value = value * share
            g_ref[i, a] = value.astype(BF16)
    scale = 1.0 / (512.0 * 64.0)
    for i in range(4):
        total = lax.dot_general(
            jnp.concatenate([tw_ref[i, a] for a in range(XTILES)], axis=1),
            jnp.concatenate([g_ref[i, a] for a in range(XTILES)], axis=1),
            (((1,), (1,)), ((), ())),
            preferred_element_type=F32,
        )
        total = total * (scale if i % 2 == 0 else -scale)
        for p in range(4):
            send_ref[pl.ds(first_row[i] + p, SOURCES, stride=16), :] = total[64 * p : 64 * p + 64]
    out_ref[...] = send_ref[...].reshape(SOURCES, 16, 128).astype(BF16)


def direct_kernel(
    pos_hbm, base_hbm, arrived_ref, weight_ref, drag_ref, masked_ref, legv_ref,
    out_ref, pos_ref, base_ref, v_ref, acc_ref, comb_ref, turned_ref, small,
):
    inputs = [
        pltpu.make_async_copy(pos_hbm, pos_ref, small.at[0]),
        pltpu.make_async_copy(base_hbm, base_ref, small.at[1]),
    ]
    for copy in inputs:
        copy.start()
    for b in range(8):
        cols = slice(128 * b, 128 * b + 128)
        weight = -weight_ref[0:1, cols]
        sides = []
        for l in range(LEVELS):
            north = (weight * drag_ref[l, 0:1, cols]) * arrived_ref[16 * l + b].astype(F32)
            south = (weight * drag_ref[l, 1:2, cols]) * arrived_ref[16 * l + 8 + b].astype(F32)
            sides.append((north + south, north - south))
        for a in range(2):
            for c in range(2):
                for pair in range(2):
                    piece = jnp.concatenate(
                        [sides[2 * pair + i][a][8 * c : 8 * c + 8] for i in range(2)], axis=0
                    )
                    row = (a * 2 + c) * 32 + pair * 16
                    v_ref[b, row : row + 16, :] = piece.astype(BF16)
    comb_ref[...] = jnp.zeros_like(comb_ref)
    lane = iota((8, 128), 1)
    offset = row_offset(iota((4, 128), 1))
    left = lane < 64
    even_rows = lane % ROWS < ROWS // 2
    for copy in inputs:
        copy.wait()

    def finish(group, part, product):
        acc_ref[part, 0:128, :] = product[:, 0:128]
        acc_ref[part, 128:256, :] = product[:, 128:256]
        for q in range(4):
            k = 4 * group + q
            rows = acc_ref[part, pl.ds(128 * (q // 2) + pos_ref[k], 16, stride=8), :]
            value = jnp.where(even_rows, rows[0:8], rows[8:16])
            if q % 2 == 0:
                value = jnp.where(left, value, pltpu.roll(pltpu.roll(value, 64, 1), 4, 0))
            else:
                value = jnp.where(left, pltpu.roll(value, 64, 1), pltpu.roll(value, 4, 0))
            live = base_ref[k] + offset < NTRUNC
            total = jnp.where(live, value[0:4] + masked_ref[pl.ds(4 * k, 4), :], 0.0)
            comb_ref[pl.ds(k, 4, stride=KPAD), :] = total

    steps = BLOCKS // 12

    def turn(step):
        for part in range(TURNED):
            group = 3 * step + part
            for i in range(2):
                for b in range(8):
                    tile = legv_ref[
                        4 * group + 2 * i : 4 * group + 2 * i + 2, :, 128 * b : 128 * b + 128
                    ]
                    turned_ref[2 * (step % 2) + part, i, 128 * b : 128 * b + 128, :] = (
                        tile.reshape(128, 128).T
                    )

    turn(0)
    for step in range(steps):
        lhs = jnp.concatenate([v_ref[b] for b in range(8)], axis=1)
        if step + 1 < steps:
            turn(step + 1)
        for part in (2, 0, 1):
            group = 3 * step + part
            if part < TURNED:
                slot = 2 * (step % 2) + part
                rhs = jnp.concatenate([turned_ref[slot, 0], turned_ref[slot, 1]], axis=1)
                product = jnp.dot(lhs, rhs, preferred_element_type=F32)
            else:
                rhs = legv_ref[4 * group : 4 * group + 4].reshape(4 * ROWS, LATS)
                product = lax.dot_general(
                    lhs, rhs, (((1,), (1,)), ((), ())), preferred_element_type=F32
                )
            finish(group, part + 3 * (step % 2), product)
    out_ref[...] = comb_ref[...].astype(BF16)


def vertical_kernel(
    own_ref, one_ref, two_ref, three_ref, gain_ref, kron_ref, coef_ref,
    out_hbm, out_ref, sems,
):
    sources = (own_ref, one_ref, two_ref, three_ref)
    both = jnp.concatenate([kron_ref[0], kron_ref[1]], axis=1)
    copies = []
    for t in range(KPAD // 8):
        stacked = jnp.concatenate(
            [
                s[KPAD * j + 8 * t : KPAD * j + 8 * t + 8, :]
                for s in sources
                for j in range(LEVELS)
            ],
            axis=0,
        )
        modal = jnp.dot(
            both, jnp.concatenate([stacked, stacked], axis=0), preferred_element_type=F32
        )
        results = [None] * LEVELS
        for a in range(ALL_LEVELS):
            scaled = modal[8 * a : 8 * a + 8] * gain_ref[a, 8 * t : 8 * t + 8, :]
            for l in range(LEVELS):
                term = coef_ref[16 * l + a : 16 * l + a + 1, :] * scaled
                results[l] = term if a == 0 else results[l] + term
        count = min(8, BLOCKS - 8 * t)
        for l in range(LEVELS):
            out_ref[pl.ds(32 * t + l, count, stride=LEVELS), :] = results[l][0:count]
        rows = pl.ds(32 * t, 4 * count)
        copies.append(pltpu.make_async_copy(out_ref.at[rows], out_hbm.at[rows], sems.at[t]))
        copies[-1].start()
    for copy in copies:
        copy.wait()


def specs(*kinds):
    spaces = {"s": pltpu.SMEM, "v": pltpu.VMEM, "h": pltpu.HBM, "a": pl.ANY}
    return [pl.BlockSpec(memory_space=spaces[k]) for k in kinds]


def in_hbm(x):
    return pltpu.with_memory_space_constraint(x, pltpu.HBM)


def on_device(
    spectral, legendre, wave_ids, block_slot, block_start, lat_weights, drag, mode_inverse,
    level_modes, depths,
):
    lev = lax.axis_index("lev").astype(jnp.int32).reshape(1)
    spec = spectral.reshape(BLOCKS * LEVELS, 128)
    outgoing, legv, masked, pos, base = pl.pallas_call(
        forward_kernel,
        in_specs=specs("h", "h", "h", "h", "h"),
        out_specs=specs("v", "v", "v", "h", "h"),
        out_shape=(
            jax.ShapeDtypeStruct((SOURCES * SENT_ROWS, 128), BF16),
            pltpu.VMEM((BLOCKS, ROWS, LATS), BF16),
            pltpu.VMEM((BLOCKS * LEVELS, 128), F32),
            jax.ShapeDtypeStruct((BLOCKS,), jnp.int32),
            jax.ShapeDtypeStruct((BLOCKS,), jnp.int32),
        ),
        scratch_shapes=[
            pltpu.SMEM((8,), jnp.int32),
            pltpu.SMEM((BLOCKS,), jnp.int32),
            pltpu.SMEM((BLOCKS,), jnp.int32),
            pltpu.SMEM((8,), jnp.int32),
            pltpu.SMEM((BLOCKS,), jnp.int32),
            pltpu.SMEM((BLOCKS,), jnp.int32),
            pltpu.VMEM((BLOCKS // 2, 128, 128), BF16),
            pltpu.VMEM((8, 128, 128), F32),
            pltpu.VMEM((SOURCES * SENT_ROWS, 128), F32),
            pltpu.SemaphoreType.DMA((CHUNKS,)),
            pltpu.SemaphoreType.DMA((6,)),
        ],
        compiler_params=pltpu.CompilerParams(vmem_limit_bytes=24 * MB),
        name="forward",
    )(*[in_hbm(x) for x in (wave_ids, block_slot, block_start, spec, legendre)])
    pairs = SENT_ROWS // 2
    incoming = lax.all_to_all(
        outgoing.reshape(SOURCES, pairs, 2, 128), "band", split_axis=0, concat_axis=0, tiled=True
    ).reshape(SOURCES * SENT_ROWS, 128)
    filtered = pl.pallas_call(
        grid_kernel,
        in_specs=specs("v"),
        out_specs=specs("v")[0],
        out_shape=jax.ShapeDtypeStruct((SOURCES, 16, 128), BF16),
        scratch_shapes=[
            pltpu.VMEM((SOURCES * SENT_ROWS, 128), F32),
            pltpu.VMEM((4, XTILES, 256, 128), BF16),
            pltpu.VMEM((4, XTILES, 128, 128), BF16),
            pltpu.VMEM((SOURCES * 16, 128), F32),
        ],
        compiler_params=pltpu.CompilerParams(vmem_limit_bytes=16 * MB),
        name="grid",
    )(incoming)
    arrived = lax.all_to_all(filtered, "band", split_axis=0, concat_axis=0, tiled=True)
    combined = pl.pallas_call(
        direct_kernel,
        in_specs=specs("h", "h", "v", "v", "v", "v", "v"),
        out_specs=specs("v")[0],
        out_shape=jax.ShapeDtypeStruct((LEVELS * KPAD, 128), BF16),
        scratch_shapes=[
            pltpu.SMEM((BLOCKS,), jnp.int32),
            pltpu.SMEM((BLOCKS,), jnp.int32),
            pltpu.VMEM((8, 128, 128), BF16),
            pltpu.VMEM((6, 256, 128), F32),
            pltpu.VMEM((LEVELS * KPAD, 128), F32),
            pltpu.VMEM((4, 2, LATS, 128), BF16),
            pltpu.SemaphoreType.DMA((2,)),
        ],
        compiler_params=pltpu.CompilerParams(vmem_limit_bytes=16 * MB),
        name="direct",
    )(pos, base, arrived, lat_weights.reshape(1, LATS), drag, masked, legv)
    others = [
        lax.ppermute(combined, "lev", [(i, (i + s) % 4) for i in range(4)]) for s in (1, 2, 3)
    ]
    late_base, combined = lax.optimization_barrier((base, combined))
    gain, kron, coef = pl.pallas_call(
        prepare_kernel,
        in_specs=specs("s", "s", "s", "s", "v"),
        out_specs=specs("v", "v", "v"),
        out_shape=(
            pltpu.VMEM((ALL_LEVELS, KPAD, 128), F32),
            pltpu.VMEM((2, 128, 128), BF16),
            pltpu.VMEM((LEVELS * ALL_LEVELS, 128), F32),
        ),
        scratch_shapes=[pltpu.VMEM((KPAD, 128), F32)],
        compiler_params=pltpu.CompilerParams(vmem_limit_bytes=24 * MB),
        name="prepare",
    )(lev, late_base, level_modes, depths, mode_inverse)
    result = pl.pallas_call(
        vertical_kernel,
        in_specs=specs("v", "v", "v", "v", "v", "v", "v"),
        out_specs=specs("h")[0],
        out_shape=jax.ShapeDtypeStruct((BLOCKS * LEVELS, 128), F32),
        scratch_shapes=[
            pltpu.VMEM((BLOCKS * LEVELS, 128), F32),
            pltpu.SemaphoreType.DMA((KPAD // 8,)),
        ],
        compiler_params=pltpu.CompilerParams(vmem_limit_bytes=16 * MB),
        name="vertical",
    )(combined, *others, gain, kron, coef)
    return result.reshape(BLOCKS, LEVELS, 128)


def solution(mesh):
    placed = (
        P("band", "lev", None),
        P("band", None, None),
        P("band"),
        P("band"),
        P("band"),
        P(),
        P("lev", None, None),
        P(),
        P(),
        P(),
    )
    return jax.shard_map(
        on_device, mesh=mesh, in_specs=placed, out_specs=P("band", "lev", None), check_vma=False
    )
```

```python
import math

import jax
import jax.numpy as jnp
from jax import lax
from jax.experimental import pallas as pl
from jax.experimental.pallas import tpu as pltpu
from jax.sharding import PartitionSpec as P

NTRUNC = 1280
NLON = 4096
BLOCKS = 84
ROWS = 64
LATS = 1024
LEVELS = 4
ALL_LEVELS = 16
SOURCES = 64
SENT_ROWS = 18
CHUNK = 12
CHUNKS = BLOCKS // CHUNK
KPAD = 88
XPAD = 1152
TURNED = (2, 1, 2, 1, 2, 2, 1)
AHEAD = 5
XTILES = XPAD // 128
F32 = jnp.float32
BF16 = jnp.bfloat16
MB = 1024 * 1024


def iota(shape, dim):
    return lax.broadcasted_iota(jnp.int32, shape, dim)


def row_offset(lane):
    r = lane % ROWS
    half = ROWS // 2
    return jnp.where(r < half, 2 * r, 2 * (r - half) + 1)


def sincos(turns):
    quarter = ((turns + 512) >> 10) & 3
    rest = ((turns + 512) & 1023) - 512
    t = rest.astype(F32) * (2.0 * math.pi / NLON)
    z = t * t
    s = t * (1.0 + z * (-1.0 / 6 + z * (1.0 / 120 + z * (-1.0 / 5040 + z * (1.0 / 362880)))))
    c = 1.0 + z * (-0.5 + z * (1.0 / 24 + z * (-1.0 / 720 + z * (1.0 / 40320))))
    swap = (quarter & 1) == 1
    cos = jnp.where(swap, s, c)
    sin = jnp.where(swap, c, s)
    cos = jnp.where((quarter == 1) | (quarter == 2), -cos, cos)
    sin = jnp.where(quarter >= 2, -sin, sin)
    return cos, sin


def forward_kernel(
    wave_hbm, slot_hbm, start_hbm, spec_hbm, leg_hbm,
    out_ref, legv_ref, masked_ref, pos_hbm, base_hbm,
    wave_ref, slot_ref, start_ref, place_ref, pos_ref, base_ref, lhs_ref, acc_ref, send_ref,
    sems, small,
):
    inputs = [
        pltpu.make_async_copy(wave_hbm, wave_ref, small.at[0]),
        pltpu.make_async_copy(slot_hbm, slot_ref, small.at[1]),
        pltpu.make_async_copy(start_hbm, start_ref, small.at[2]),
        pltpu.make_async_copy(spec_hbm, masked_ref, small.at[3]),
    ]
    for copy in inputs:
        copy.start()
    copies = [
        pltpu.make_async_copy(
            leg_hbm.at[pl.ds(c * CHUNK, CHUNK)], legv_ref.at[pl.ds(c * CHUNK, CHUNK)], sems.at[c]
        )
        for c in range(CHUNKS)
    ]
    for c in range(AHEAD):
        copies[c].start(priority=c % 2)
    for copy in inputs:
        copy.wait()
    lane = iota((8, 128), 1)
    sub = iota((8, 128), 0)
    offset = row_offset(lane)
    left = lane < 64
    upper = sub < 4
    sign = jnp.where(lane % ROWS < ROWS // 2, 1.0, -1.0).astype(F32)

    waves = [wave_ref[s] for s in range(8)]
    keys = [jnp.where(w % 2 == 1, 2 * NTRUNC - 1 - w, w) for w in waves]
    places = []
    for s in range(8):
        place = jnp.int32(0)
        for other in range(8):
            if other != s:
                place = place + (keys[other] < keys[s]).astype(jnp.int32)
        place_ref[s] = place
        places.append(place)
    ids = jnp.zeros((8, 128), jnp.int32)
    for s in range(8):
        ids = jnp.where(lane // 32 == places[s], waves[s], ids)
    ids = jnp.where(sub == 0, ids >> 4, ids & 15).astype(F32)

    def index(k, carry):
        slot = slot_ref[k]
        pos_ref[k] = place_ref[slot]
        base_ref[k] = wave_ref[slot] + start_ref[k]
        return carry

    lax.fori_loop(0, BLOCKS, index, 0, unroll=12)
    results = [
        pltpu.make_async_copy(pos_ref, pos_hbm, small.at[4]),
        pltpu.make_async_copy(base_ref, base_hbm, small.at[5]),
    ]
    for copy in results:
        copy.start()

    def build(j, carry):
        k0 = 2 * j
        degree = jnp.where(upper, base_ref[k0], base_ref[k0 + 1]) + offset
        here = pl.ds(pl.multiple_of(8 * j, 8), 8)
        own = jnp.where(degree < NTRUNC, masked_ref[here, :], 0.0)
        masked_ref[here, :] = own
        turned = pltpu.roll(own, 64, 1)
        parts = (
            jnp.where(left, own, pltpu.roll(turned, 4, 0)),
            jnp.where(left, turned, pltpu.roll(own, 4, 0)),
        )
        match = jnp.where(left, pos_ref[k0], pos_ref[k0 + 1]) == sub
        for l in range(LEVELS):
            north = jnp.concatenate(
                [
                    jnp.where(match, jnp.broadcast_to(p[l : l + 1], (8, 128)), 0.0)
                    for p in parts
                ],
                axis=0,
            )
            south = north * jnp.concatenate([sign, sign], axis=0)
            lhs_ref[j, 32 * l : 32 * l + 16, :] = north.astype(BF16)
            lhs_ref[j, 32 * l + 16 : 32 * l + 32, :] = south.astype(BF16)
        return carry

    half = CHUNK // 2

    def build_chunk(c):
        lax.fori_loop(c * half, (c + 1) * half, build, 0, unroll=half)

    build_chunk(0)
    for c in range(CHUNKS):
        copies[c].wait()
        if c + AHEAD < CHUNKS:
            copies[c + AHEAD].start(priority=(c + AHEAD) % 2)
        if c + 1 < CHUNKS:
            build_chunk(c + 1)
        lhs = jnp.concatenate([lhs_ref[c * half + i] for i in range(half)], axis=1)
        for n in range(LATS // 256):
            rhs = legv_ref[c * CHUNK : (c + 1) * CHUNK, :, 256 * n : 256 * n + 256]
            part = jnp.dot(lhs, rhs.reshape(CHUNK * ROWS, 256), preferred_element_type=F32)
            for i in range(2):
                b = 2 * n + i
                piece = part[:, 128 * i : 128 * i + 128]
                if c > 0:
                    piece = piece + acc_ref[b]
                if c + 1 < CHUNKS:
                    acc_ref[b] = piece
                else:
                    for g in range(8):
                        row = SENT_ROWS * (8 * g + b)
                        send_ref[row : row + 16, :] = piece[16 * g : 16 * g + 16]
                        send_ref[row + 16 : row + 18, :] = ids[0:2]
    out_ref[...] = send_ref[...].astype(BF16)
    for copy in results:
        copy.wait()


def prepare_kernel(
    lev_ref, base_ref, level_ref, depth_ref, mode_ref,
    gain_ref, kron_ref, coef_ref, growth_ref,
):
    lev = lev_ref[0]
    row_pick = (iota((128, ALL_LEVELS), 0) // 8 == iota((128, ALL_LEVELS), 1)).astype(F32)
    col = iota((ALL_LEVELS, 128), 1) // 8
    source_level = ((lev - col // LEVELS) & 3) * LEVELS + col % LEVELS
    col_pick = (iota((ALL_LEVELS, 128), 0) == source_level).astype(F32)
    high = lax.Precision.HIGHEST
    wide = jnp.dot(jnp.dot(row_pick, mode_ref[...], precision=high), col_pick, precision=high)
    wide = jnp.where(iota((128, 128), 0) % 8 == iota((128, 128), 1) % 8, wide, 0.0)
    wide_high = wide.astype(BF16)
    kron_ref[0] = wide_high
    kron_ref[1] = (wide - wide_high.astype(F32)).astype(BF16)

    growth_ref[...] = jnp.zeros_like(growth_ref)
    one = row_offset(iota((1, 128), 1))

    def grow(k, carry):
        degree = (base_ref[k] + one).astype(F32)
        growth_ref[pl.ds(k, 1), :] = degree * (degree + 1.0) / (NTRUNC * NTRUNC)
        return carry

    lax.fori_loop(0, BLOCKS, grow, 0, unroll=12)
    for a in range(ALL_LEVELS):
        gain_ref[a] = 1.0 / (1.0 + depth_ref[a] * growth_ref[...])
        for l in range(LEVELS):
            coef_ref[16 * l + a : 16 * l + a + 1, :] = jnp.full(
                (1, 128), level_ref[lev * LEVELS + l, a], F32
            )


def grid_kernel(in_ref, out_ref, recv_ref, tw_ref, g_ref, send_ref):
    recv_ref[...] = in_ref[...].astype(F32)

    def rows_of(j):
        return recv_ref[pl.ds(j, SOURCES, stride=SENT_ROWS), :]

    lane = iota((32, 128), 1)
    lane8 = iota((8, 128), 1)
    shift = [sincos(((NTRUNC - 1) * (128 * a + lane8)) & (NLON - 1)) for a in range(XTILES)]
    ids = rows_of(16) * 16.0 + rows_of(17)

    for p in range(4):
        whole = jnp.broadcast_to(ids[:, 32 * p : 32 * p + 1], (SOURCES, 128)).astype(jnp.int32)
        for half in range(2):
            wave = whole[32 * half : 32 * half + 32]
            rows = slice(64 * p + 32 * half, 64 * p + 32 * half + 32)
            cos, sin = sincos((wave * lane) & (NLON - 1))
            step_cos, step_sin = sincos((wave * 128) & (NLON - 1))
            for a in range(XTILES):
                c1 = jnp.concatenate([shift[a][0]] * 4, axis=0)
                s1 = jnp.concatenate([shift[a][1]] * 4, axis=0)
                tw_ref[0, a, rows, :] = cos.astype(BF16)
                tw_ref[3, a, rows, :] = (s1 * cos - c1 * sin).astype(BF16)
                if a + 1 < XTILES:
                    tw_ref[1, a, rows, :] = sin.astype(BF16)
                    tw_ref[2, a, rows, :] = (c1 * cos + s1 * sin).astype(BF16)
                if a + 1 < XTILES:
                    cos, sin = cos * step_cos - sin * step_sin, sin * step_cos + cos * step_sin

    first_row = (0, 8, 4, 12)
    spectra = [
        jnp.concatenate([rows_of(f + p) for p in range(4)], axis=0).T.astype(BF16)
        for f in first_row
    ]
    for a in range(XTILES - 1):
        ce, se, co, so = [
            jnp.dot(spectra[i], tw_ref[i, a], preferred_element_type=F32) for i in range(4)
        ]
        minus, plus = ce - se, ce + se
        odd_minus, odd_plus = co - so, co + so
        f1, f2, f3, f4 = [
            v * jnp.abs(v)
            for v in (minus + odd_minus, minus - odd_minus, plus + odd_plus, plus - odd_plus)
        ]
        s12, d12, s34, d34 = f1 + f2, f1 - f2, f3 + f4, f3 - f4
        folded = (s12 + s34, s12 - s34, d12 + d34, d12 - d34)
        for i in range(4):
            value = folded[i]
            if a == 0:
                value = value * jnp.where(iota((1, 128), 1) == 0, 0.5, 1.0)
            g_ref[i, a] = value.astype(BF16)
    last = XTILES - 1
    ce, so = [jnp.dot(spectra[i], tw_ref[i, last], preferred_element_type=F32) for i in (0, 3)]
    f1, f2 = [v * jnp.abs(v) for v in (ce - so, ce + so)]
    only = jnp.where(iota((1, 128), 1) == 0, 1.0, 0.0)
    g_ref[0, last] = ((f1 + f2) * only).astype(BF16)
    g_ref[3, last] = ((f1 - f2) * only).astype(BF16)
    scale = 1.0 / (512.0 * 64.0)
    for i in range(4):
        total = lax.dot_general(
            jnp.concatenate([tw_ref[i, a] for a in range(last)], axis=1),
            jnp.concatenate([g_ref[i, a] for a in range(last)], axis=1),
            (((1,), (1,)), ((), ())),
            preferred_element_type=F32,
        )
        if i in (0, 3):
            total = total + lax.dot_general(
                tw_ref[i, last],
                g_ref[i, last],
                (((1,), (1,)), ((), ())),
                preferred_element_type=F32,
            )
        total = total * (scale if i % 2 == 0 else -scale)
        for p in range(4):
            send_ref[pl.ds(first_row[i] + p, SOURCES, stride=16), :] = total[64 * p : 64 * p + 64]
    out_ref[...] = send_ref[...].reshape(SOURCES, 16, 128).astype(BF16)


def direct_kernel(
    pos_hbm, base_hbm, arrived_ref, weight_ref, drag_ref, masked_ref, legv_ref,
    out_ref, pos_ref, base_ref, v_ref, acc_ref, comb_ref, turned_ref, small,
):
    inputs = [
        pltpu.make_async_copy(pos_hbm, pos_ref, small.at[0]),
        pltpu.make_async_copy(base_hbm, base_ref, small.at[1]),
    ]
    for copy in inputs:
        copy.start()
    steps = BLOCKS // 12

    def turn(step):
        for part in range(TURNED[step]):
            group = 3 * step + part
            for i in range(2):
                for b in range(8):
                    tile = legv_ref[
                        4 * group + 2 * i : 4 * group + 2 * i + 2, :, 128 * b : 128 * b + 128
                    ]
                    turned_ref[2 * (step % 2) + part, i, 128 * b : 128 * b + 128, :] = (
                        tile.reshape(128, 128).T
                    )

    turn(0)
    for b in range(8):
        cols = slice(128 * b, 128 * b + 128)
        weight = -weight_ref[0:1, cols]
        sides = []
        for l in range(LEVELS):
            north = (weight * drag_ref[l, 0:1, cols]) * arrived_ref[16 * l + b].astype(F32)
            south = (weight * drag_ref[l, 1:2, cols]) * arrived_ref[16 * l + 8 + b].astype(F32)
            sides.append((north + south, north - south))
        for a in range(2):
            for c in range(2):
                for pair in range(2):
                    piece = jnp.concatenate(
                        [sides[2 * pair + i][a][8 * c : 8 * c + 8] for i in range(2)], axis=0
                    )
                    row = (a * 2 + c) * 32 + pair * 16
                    v_ref[b, row : row + 16, :] = piece.astype(BF16)
    comb_ref[...] = jnp.zeros_like(comb_ref)
    lane = iota((8, 128), 1)
    offset = row_offset(iota((4, 128), 1))
    left = lane < 64
    even_rows = lane % ROWS < ROWS // 2
    for copy in inputs:
        copy.wait()

    def finish(group, part, product):
        acc_ref[part, 0:128, :] = product[:, 0:128]
        acc_ref[part, 128:256, :] = product[:, 128:256]
        for q in range(4):
            k = 4 * group + q
            rows = acc_ref[part, pl.ds(128 * (q // 2) + pos_ref[k], 16, stride=8), :]
            value = jnp.where(even_rows, rows[0:8], rows[8:16])
            if q % 2 == 0:
                value = jnp.where(left, value, pltpu.roll(pltpu.roll(value, 64, 1), 4, 0))
            else:
                value = jnp.where(left, pltpu.roll(value, 64, 1), pltpu.roll(value, 4, 0))
            live = base_ref[k] + offset < NTRUNC
            total = jnp.where(live, value[0:4] + masked_ref[pl.ds(4 * k, 4), :], 0.0)
            comb_ref[pl.ds(k, 4, stride=KPAD), :] = total

    for step in range(steps):
        lhs = jnp.concatenate([v_ref[b] for b in range(8)], axis=1)
        if step + 1 < steps:
            turn(step + 1)
        for part in (2, 0, 1):
            group = 3 * step + part
            if part < TURNED[step]:
                slot = 2 * (step % 2) + part
                rhs = jnp.concatenate([turned_ref[slot, 0], turned_ref[slot, 1]], axis=1)
                product = jnp.dot(lhs, rhs, preferred_element_type=F32)
            else:
                rhs = legv_ref[4 * group : 4 * group + 4].reshape(4 * ROWS, LATS)
                product = lax.dot_general(
                    lhs, rhs, (((1,), (1,)), ((), ())), preferred_element_type=F32
                )
            finish(group, part + 3 * (step % 2), product)
    out_ref[...] = comb_ref[...].astype(BF16)


def vertical_kernel(
    own_ref, one_ref, two_ref, three_ref, gain_ref, kron_ref, coef_ref,
    out_hbm, out_ref, sems,
):
    sources = (own_ref, one_ref, two_ref, three_ref)
    both = jnp.concatenate([kron_ref[0], kron_ref[1]], axis=1)
    copies = []
    for t in range(KPAD // 8):
        stacked = jnp.concatenate(
            [
                s[KPAD * j + 8 * t : KPAD * j + 8 * t + 8, :]
                for s in sources
                for j in range(LEVELS)
            ],
            axis=0,
        )
        modal = jnp.dot(
            both, jnp.concatenate([stacked, stacked], axis=0), preferred_element_type=F32
        )
        results = [None] * LEVELS
        for a in range(ALL_LEVELS):
            scaled = modal[8 * a : 8 * a + 8] * gain_ref[a, 8 * t : 8 * t + 8, :]
            for l in range(LEVELS):
                term = coef_ref[16 * l + a : 16 * l + a + 1, :] * scaled
                results[l] = term if a == 0 else results[l] + term
        count = min(8, BLOCKS - 8 * t)
        for l in range(LEVELS):
            out_ref[pl.ds(32 * t + l, count, stride=LEVELS), :] = results[l][0:count]
        rows = pl.ds(32 * t, 4 * count)
        copies.append(pltpu.make_async_copy(out_ref.at[rows], out_hbm.at[rows], sems.at[t]))
        copies[-1].start()
    for copy in copies:
        copy.wait()


def specs(*kinds):
    spaces = {"s": pltpu.SMEM, "v": pltpu.VMEM, "h": pltpu.HBM, "a": pl.ANY}
    return [pl.BlockSpec(memory_space=spaces[k]) for k in kinds]


def in_hbm(x):
    return pltpu.with_memory_space_constraint(x, pltpu.HBM)


def on_device(
    spectral, legendre, wave_ids, block_slot, block_start, lat_weights, drag, mode_inverse,
    level_modes, depths,
):
    lev = lax.axis_index("lev").astype(jnp.int32).reshape(1)
    spec = spectral.reshape(BLOCKS * LEVELS, 128)
    outgoing, legv, masked, pos, base = pl.pallas_call(
        forward_kernel,
        in_specs=specs("h", "h", "h", "h", "h"),
        out_specs=specs("v", "v", "v", "h", "h"),
        out_shape=(
            jax.ShapeDtypeStruct((SOURCES * SENT_ROWS, 128), BF16),
            pltpu.VMEM((BLOCKS, ROWS, LATS), BF16),
            pltpu.VMEM((BLOCKS * LEVELS, 128), F32),
            jax.ShapeDtypeStruct((BLOCKS,), jnp.int32),
            jax.ShapeDtypeStruct((BLOCKS,), jnp.int32),
        ),
        scratch_shapes=[
            pltpu.SMEM((8,), jnp.int32),
            pltpu.SMEM((BLOCKS,), jnp.int32),
            pltpu.SMEM((BLOCKS,), jnp.int32),
            pltpu.SMEM((8,), jnp.int32),
            pltpu.SMEM((BLOCKS,), jnp.int32),
            pltpu.SMEM((BLOCKS,), jnp.int32),
            pltpu.VMEM((BLOCKS // 2, 128, 128), BF16),
            pltpu.VMEM((8, 128, 128), F32),
            pltpu.VMEM((SOURCES * SENT_ROWS, 128), F32),
            pltpu.SemaphoreType.DMA((CHUNKS,)),
            pltpu.SemaphoreType.DMA((6,)),
        ],
        compiler_params=pltpu.CompilerParams(vmem_limit_bytes=24 * MB),
        name="forward",
    )(*[in_hbm(x) for x in (wave_ids, block_slot, block_start, spec, legendre)])
    pairs = SENT_ROWS // 2
    incoming = lax.all_to_all(
        outgoing.reshape(SOURCES, pairs, 2, 128), "band", split_axis=0, concat_axis=0, tiled=True
    ).reshape(SOURCES * SENT_ROWS, 128)
    filtered = pl.pallas_call(
        grid_kernel,
        in_specs=specs("v"),
        out_specs=specs("v")[0],
        out_shape=jax.ShapeDtypeStruct((SOURCES, 16, 128), BF16),
        scratch_shapes=[
            pltpu.VMEM((SOURCES * SENT_ROWS, 128), F32),
            pltpu.VMEM((4, XTILES, 256, 128), BF16),
            pltpu.VMEM((4, XTILES, 128, 128), BF16),
            pltpu.VMEM((SOURCES * 16, 128), F32),
        ],
        compiler_params=pltpu.CompilerParams(vmem_limit_bytes=16 * MB),
        name="grid",
    )(incoming)
    arrived = lax.all_to_all(filtered, "band", split_axis=0, concat_axis=0, tiled=True)
    combined = pl.pallas_call(
        direct_kernel,
        in_specs=specs("h", "h", "v", "v", "v", "v", "v"),
        out_specs=specs("v")[0],
        out_shape=jax.ShapeDtypeStruct((LEVELS * KPAD, 128), BF16),
        scratch_shapes=[
            pltpu.SMEM((BLOCKS,), jnp.int32),
            pltpu.SMEM((BLOCKS,), jnp.int32),
            pltpu.VMEM((8, 128, 128), BF16),
            pltpu.VMEM((6, 256, 128), F32),
            pltpu.VMEM((LEVELS * KPAD, 128), F32),
            pltpu.VMEM((4, 2, LATS, 128), BF16),
            pltpu.SemaphoreType.DMA((2,)),
        ],
        compiler_params=pltpu.CompilerParams(vmem_limit_bytes=16 * MB),
        name="direct",
    )(pos, base, arrived, lat_weights.reshape(1, LATS), drag, masked, legv)
    others = [
        lax.ppermute(combined, "lev", [(i, (i + s) % 4) for i in range(4)]) for s in (1, 2, 3)
    ]
    late_base, combined = lax.optimization_barrier((base, combined))
    gain, kron, coef = pl.pallas_call(
        prepare_kernel,
        in_specs=specs("s", "s", "s", "s", "v"),
        out_specs=specs("v", "v", "v"),
        out_shape=(
            pltpu.VMEM((ALL_LEVELS, KPAD, 128), F32),
            pltpu.VMEM((2, 128, 128), BF16),
            pltpu.VMEM((LEVELS * ALL_LEVELS, 128), F32),
        ),
        scratch_shapes=[pltpu.VMEM((KPAD, 128), F32)],
        compiler_params=pltpu.CompilerParams(vmem_limit_bytes=24 * MB),
        name="prepare",
    )(lev, late_base, level_modes, depths, mode_inverse)
    result = pl.pallas_call(
        vertical_kernel,
        in_specs=specs("v", "v", "v", "v", "v", "v", "v"),
        out_specs=specs("h")[0],
        out_shape=jax.ShapeDtypeStruct((BLOCKS * LEVELS, 128), F32),
        scratch_shapes=[
            pltpu.VMEM((BLOCKS * LEVELS, 128), F32),
            pltpu.SemaphoreType.DMA((KPAD // 8,)),
        ],
        compiler_params=pltpu.CompilerParams(vmem_limit_bytes=16 * MB),
        name="vertical",
    )(combined, *others, gain, kron, coef)
    return result.reshape(BLOCKS, LEVELS, 128)


def solution(mesh):
    placed = (
        P("band", "lev", None),
        P("band", None, None),
        P("band"),
        P("band"),
        P("band"),
        P(),
        P("lev", None, None),
        P(),
        P(),
        P(),
    )
    return jax.shard_map(
        on_device, mesh=mesh, in_specs=placed, out_specs=P("band", "lev", None), check_vma=False
    )
```

```python
import math

import jax
import jax.numpy as jnp
from jax import lax
from jax.experimental import pallas as pl
from jax.experimental.pallas import tpu as pltpu
from jax.sharding import PartitionSpec as P

NTRUNC = 1280
NLON = 4096
BLOCKS = 84
ROWS = 64
LATS = 1024
LEVELS = 4
ALL_LEVELS = 16
SOURCES = 64
SENT_ROWS = 18
CHUNK = 12
CHUNKS = BLOCKS // CHUNK
KPAD = 88
XPAD = 1152
TURNED = (2, 1, 2, 1, 2, 2, 1)
AHEAD = 5
OUT_TILES = (3, 6, 8, 10)
XTILES = XPAD // 128
F32 = jnp.float32
BF16 = jnp.bfloat16
MB = 1024 * 1024


def iota(shape, dim):
    return lax.broadcasted_iota(jnp.int32, shape, dim)


def row_offset(lane):
    r = lane % ROWS
    half = ROWS // 2
    return jnp.where(r < half, 2 * r, 2 * (r - half) + 1)


def sincos(turns):
    quarter = ((turns + 512) >> 10) & 3
    rest = ((turns + 512) & 1023) - 512
    t = rest.astype(F32) * (2.0 * math.pi / NLON)
    z = t * t
    s = t * (1.0 + z * (-1.0 / 6 + z * (1.0 / 120 + z * (-1.0 / 5040 + z * (1.0 / 362880)))))
    c = 1.0 + z * (-0.5 + z * (1.0 / 24 + z * (-1.0 / 720 + z * (1.0 / 40320))))
    swap = (quarter & 1) == 1
    cos = jnp.where(swap, s, c)
    sin = jnp.where(swap, c, s)
    cos = jnp.where((quarter == 1) | (quarter == 2), -cos, cos)
    sin = jnp.where(quarter >= 2, -sin, sin)
    return cos, sin


def forward_kernel(
    wave_hbm, slot_hbm, start_hbm, spec_hbm, leg_hbm,
    out_ref, legv_ref, masked_ref, pos_hbm, base_hbm,
    wave_ref, slot_ref, start_ref, place_ref, pos_ref, base_ref, lhs_ref, acc_ref, send_ref,
    sems, small,
):
    inputs = [
        pltpu.make_async_copy(wave_hbm, wave_ref, small.at[0]),
        pltpu.make_async_copy(slot_hbm, slot_ref, small.at[1]),
        pltpu.make_async_copy(start_hbm, start_ref, small.at[2]),
        pltpu.make_async_copy(spec_hbm, masked_ref, small.at[3]),
    ]
    for copy in inputs:
        copy.start()
    copies = [
        pltpu.make_async_copy(
            leg_hbm.at[pl.ds(c * CHUNK, CHUNK)], legv_ref.at[pl.ds(c * CHUNK, CHUNK)], sems.at[c]
        )
        for c in range(CHUNKS)
    ]
    for c in range(AHEAD):
        copies[c].start(priority=c % 2)
    for copy in inputs:
        copy.wait()
    lane = iota((8, 128), 1)
    sub = iota((8, 128), 0)
    offset = row_offset(lane)
    left = lane < 64
    upper = sub < 4
    sign = jnp.where(lane % ROWS < ROWS // 2, 1.0, -1.0).astype(F32)

    waves = [wave_ref[s] for s in range(8)]
    keys = [jnp.where(w % 2 == 1, 2 * NTRUNC - 1 - w, w) for w in waves]
    places = []
    for s in range(8):
        place = jnp.int32(0)
        for other in range(8):
            if other != s:
                place = place + (keys[other] < keys[s]).astype(jnp.int32)
        place_ref[s] = place
        places.append(place)
    ids = jnp.zeros((8, 128), jnp.int32)
    for s in range(8):
        ids = jnp.where(lane // 32 == places[s], waves[s], ids)
    ids = jnp.where(sub == 0, ids >> 4, ids & 15).astype(F32)

    def index(k, carry):
        slot = slot_ref[k]
        pos_ref[k] = place_ref[slot]
        base_ref[k] = wave_ref[slot] + start_ref[k]
        return carry

    lax.fori_loop(0, BLOCKS, index, 0, unroll=12)
    results = [
        pltpu.make_async_copy(pos_ref, pos_hbm, small.at[4]),
        pltpu.make_async_copy(base_ref, base_hbm, small.at[5]),
    ]
    for copy in results:
        copy.start()

    def build(j, carry):
        k0 = 2 * j
        degree = jnp.where(upper, base_ref[k0], base_ref[k0 + 1]) + offset
        here = pl.ds(pl.multiple_of(8 * j, 8), 8)
        own = jnp.where(degree < NTRUNC, masked_ref[here, :], 0.0)
        masked_ref[here, :] = own
        turned = pltpu.roll(own, 64, 1)
        parts = (
            jnp.where(left, own, pltpu.roll(turned, 4, 0)),
            jnp.where(left, turned, pltpu.roll(own, 4, 0)),
        )
        match = jnp.where(left, pos_ref[k0], pos_ref[k0 + 1]) == sub
        for l in range(LEVELS):
            north = jnp.concatenate(
                [
                    jnp.where(match, jnp.broadcast_to(p[l : l + 1], (8, 128)), 0.0)
                    for p in parts
                ],
                axis=0,
            )
            south = north * jnp.concatenate([sign, sign], axis=0)
            lhs_ref[j, 32 * l : 32 * l + 16, :] = north.astype(BF16)
            lhs_ref[j, 32 * l + 16 : 32 * l + 32, :] = south.astype(BF16)
        return carry

    half = CHUNK // 2

    def build_chunk(c):
        lax.fori_loop(c * half, (c + 1) * half, build, 0, unroll=half)

    build_chunk(0)
    for c in range(CHUNKS):
        copies[c].wait()
        if c + AHEAD < CHUNKS:
            copies[c + AHEAD].start(priority=(c + AHEAD) % 2)
        if c + 1 < CHUNKS:
            build_chunk(c + 1)
        lhs = jnp.concatenate([lhs_ref[c * half + i] for i in range(half)], axis=1)
        for n in range(LATS // 256):
            rhs = legv_ref[c * CHUNK : (c + 1) * CHUNK, :, 256 * n : 256 * n + 256]
            part = jnp.dot(lhs, rhs.reshape(CHUNK * ROWS, 256), preferred_element_type=F32)
            for i in range(2):
                b = 2 * n + i
                piece = part[:, 128 * i : 128 * i + 128]
                if c > 0:
                    piece = piece + acc_ref[b]
                if c + 1 < CHUNKS:
                    acc_ref[b] = piece
                else:
                    for g in range(8):
                        row = SENT_ROWS * (8 * g + b)
                        send_ref[row : row + 16, :] = piece[16 * g : 16 * g + 16]
                        send_ref[row + 16 : row + 18, :] = ids[0:2]
    out_ref[...] = send_ref[...].astype(BF16)
    for copy in results:
        copy.wait()


def prepare_kernel(
    lev_ref, base_ref, level_ref, depth_ref, mode_ref,
    gain_ref, kron_ref, coef_ref, growth_ref,
):
    lev = lev_ref[0]
    row_pick = (iota((128, ALL_LEVELS), 0) // 8 == iota((128, ALL_LEVELS), 1)).astype(F32)
    col = iota((ALL_LEVELS, 128), 1) // 8
    source_level = ((lev - col // LEVELS) & 3) * LEVELS + col % LEVELS
    col_pick = (iota((ALL_LEVELS, 128), 0) == source_level).astype(F32)
    high = lax.Precision.HIGHEST
    wide = jnp.dot(jnp.dot(row_pick, mode_ref[...], precision=high), col_pick, precision=high)
    wide = jnp.where(iota((128, 128), 0) % 8 == iota((128, 128), 1) % 8, wide, 0.0)
    wide_high = wide.astype(BF16)
    kron_ref[0] = wide_high
    kron_ref[1] = (wide - wide_high.astype(F32)).astype(BF16)

    growth_ref[...] = jnp.zeros_like(growth_ref)
    one = row_offset(iota((1, 128), 1))

    def grow(k, carry):
        degree = (base_ref[k] + one).astype(F32)
        growth_ref[pl.ds(k, 1), :] = degree * (degree + 1.0) / (NTRUNC * NTRUNC)
        return carry

    lax.fori_loop(0, BLOCKS, grow, 0, unroll=12)
    for a in range(ALL_LEVELS):
        gain_ref[a] = 1.0 / (1.0 + depth_ref[a] * growth_ref[...])
        for l in range(LEVELS):
            coef_ref[16 * l + a : 16 * l + a + 1, :] = jnp.full(
                (1, 128), level_ref[lev * LEVELS + l, a], F32
            )


def grid_kernel(in_ref, out_ref, recv_ref, tw_ref, g_ref, send_ref):
    recv_ref[...] = in_ref[...].astype(F32)

    def rows_of(j):
        return recv_ref[pl.ds(j, SOURCES, stride=SENT_ROWS), :]

    lane = iota((32, 128), 1)
    lane8 = iota((8, 128), 1)
    shift = [sincos(((NTRUNC - 1) * (128 * a + lane8)) & (NLON - 1)) for a in range(XTILES)]
    ids = rows_of(16) * 16.0 + rows_of(17)

    for p in range(4):
        whole = jnp.broadcast_to(ids[:, 32 * p : 32 * p + 1], (SOURCES, 128)).astype(jnp.int32)
        for half in range(2):
            wave = whole[32 * half : 32 * half + 32]
            rows = slice(64 * p + 32 * half, 64 * p + 32 * half + 32)
            cos, sin = sincos((wave * lane) & (NLON - 1))
            step_cos, step_sin = sincos((wave * 128) & (NLON - 1))
            for a in range(XTILES):
                c1 = jnp.concatenate([shift[a][0]] * 4, axis=0)
                s1 = jnp.concatenate([shift[a][1]] * 4, axis=0)
                tw_ref[0, a, rows, :] = cos.astype(BF16)
                tw_ref[3, a, rows, :] = (s1 * cos - c1 * sin).astype(BF16)
                if a + 1 < XTILES:
                    tw_ref[1, a, rows, :] = sin.astype(BF16)
                    tw_ref[2, a, rows, :] = (c1 * cos + s1 * sin).astype(BF16)
                if a + 1 < XTILES:
                    cos, sin = cos * step_cos - sin * step_sin, sin * step_cos + cos * step_sin

    first_row = (0, 8, 4, 12)
    spectra = [
        jnp.concatenate([rows_of(f + p) for p in range(4)], axis=0).T.astype(BF16)
        for f in first_row
    ]
    for a in range(XTILES - 1):
        ce, se, co, so = [
            jnp.dot(spectra[i], tw_ref[i, a], preferred_element_type=F32) for i in range(4)
        ]
        minus, plus = ce - se, ce + se
        odd_minus, odd_plus = co - so, co + so
        f1, f2, f3, f4 = [
            v * jnp.abs(v)
            for v in (minus + odd_minus, minus - odd_minus, plus + odd_plus, plus - odd_plus)
        ]
        s12, d12, s34, d34 = f1 + f2, f1 - f2, f3 + f4, f3 - f4
        folded = (s12 + s34, s12 - s34, d12 + d34, d12 - d34)
        for i in range(4):
            value = folded[i]
            if a == 0:
                value = value * jnp.where(iota((1, 128), 1) == 0, 0.5, 1.0)
            g_ref[i, a] = value.astype(BF16)
    last = XTILES - 1
    ce, so = [jnp.dot(spectra[i], tw_ref[i, last], preferred_element_type=F32) for i in (0, 3)]
    f1, f2 = [v * jnp.abs(v) for v in (ce - so, ce + so)]
    only = jnp.where(iota((1, 128), 1) == 0, 1.0, 0.0)
    g_ref[0, last] = ((f1 + f2) * only).astype(BF16)
    g_ref[3, last] = ((f1 - f2) * only).astype(BF16)
    scale = 1.0 / (512.0 * 64.0)
    for i in range(4):
        total = lax.dot_general(
            jnp.concatenate([tw_ref[i, a] for a in range(last)], axis=1),
            jnp.concatenate([g_ref[i, a] for a in range(last)], axis=1),
            (((1,), (1,)), ((), ())),
            preferred_element_type=F32,
        )
        if i in (0, 3):
            total = total + lax.dot_general(
                tw_ref[i, last],
                g_ref[i, last],
                (((1,), (1,)), ((), ())),
                preferred_element_type=F32,
            )
        total = total * (scale if i % 2 == 0 else -scale)
        for p in range(4):
            send_ref[pl.ds(first_row[i] + p, SOURCES, stride=16), :] = total[64 * p : 64 * p + 64]
    out_ref[...] = send_ref[...].reshape(SOURCES, 16, 128).astype(BF16)


def direct_kernel(
    pos_hbm, base_hbm, arrived_ref, weight_ref, drag_ref, masked_ref, legv_ref,
    out_ref, pos_ref, base_ref, v_ref, acc_ref, comb_ref, turned_ref, small,
):
    inputs = [
        pltpu.make_async_copy(pos_hbm, pos_ref, small.at[0]),
        pltpu.make_async_copy(base_hbm, base_ref, small.at[1]),
    ]
    for copy in inputs:
        copy.start()
    steps = BLOCKS // 12

    def turn(step):
        for part in range(TURNED[step]):
            group = 3 * step + part
            for i in range(2):
                for b in range(8):
                    tile = legv_ref[
                        4 * group + 2 * i : 4 * group + 2 * i + 2, :, 128 * b : 128 * b + 128
                    ]
                    turned_ref[2 * (step % 2) + part, i, 128 * b : 128 * b + 128, :] = (
                        tile.reshape(128, 128).T
                    )

    turn(0)
    for b in range(8):
        cols = slice(128 * b, 128 * b + 128)
        weight = -weight_ref[0:1, cols]
        sides = []
        for l in range(LEVELS):
            north = (weight * drag_ref[l, 0:1, cols]) * arrived_ref[16 * l + b].astype(F32)
            south = (weight * drag_ref[l, 1:2, cols]) * arrived_ref[16 * l + 8 + b].astype(F32)
            sides.append((north + south, north - south))
        for a in range(2):
            for c in range(2):
                for pair in range(2):
                    piece = jnp.concatenate(
                        [sides[2 * pair + i][a][8 * c : 8 * c + 8] for i in range(2)], axis=0
                    )
                    row = (a * 2 + c) * 32 + pair * 16
                    v_ref[b, row : row + 16, :] = piece.astype(BF16)
    comb_ref[...] = jnp.zeros_like(comb_ref)
    lane = iota((8, 128), 1)
    offset = row_offset(iota((4, 128), 1))
    left = lane < 64
    even_rows = lane % ROWS < ROWS // 2
    for copy in inputs:
        copy.wait()

    def finish(group, part, product):
        acc_ref[part, 0:128, :] = product[:, 0:128]
        acc_ref[part, 128:256, :] = product[:, 128:256]
        for q in range(4):
            k = 4 * group + q
            rows = acc_ref[part, pl.ds(128 * (q // 2) + pos_ref[k], 16, stride=8), :]
            value = jnp.where(even_rows, rows[0:8], rows[8:16])
            if q % 2 == 0:
                value = jnp.where(left, value, pltpu.roll(pltpu.roll(value, 64, 1), 4, 0))
            else:
                value = jnp.where(left, pltpu.roll(value, 64, 1), pltpu.roll(value, 4, 0))
            live = base_ref[k] + offset < NTRUNC
            total = jnp.where(live, value[0:4] + masked_ref[pl.ds(4 * k, 4), :], 0.0)
            comb_ref[pl.ds(k, 4, stride=KPAD), :] = total

    for step in range(steps):
        lhs = jnp.concatenate([v_ref[b] for b in range(8)], axis=1)
        if step + 1 < steps:
            turn(step + 1)
        for part in (2, 0, 1):
            group = 3 * step + part
            if part < TURNED[step]:
                slot = 2 * (step % 2) + part
                rhs = jnp.concatenate([turned_ref[slot, 0], turned_ref[slot, 1]], axis=1)
                product = jnp.dot(lhs, rhs, preferred_element_type=F32)
            else:
                rhs = legv_ref[4 * group : 4 * group + 4].reshape(4 * ROWS, LATS)
                product = lax.dot_general(
                    lhs, rhs, (((1,), (1,)), ((), ())), preferred_element_type=F32
                )
            finish(group, part + 3 * (step % 2), product)
    out_ref[...] = comb_ref[...].astype(BF16)


def vertical_kernel(
    own_ref, one_ref, two_ref, three_ref, gain_ref, kron_ref, coef_ref,
    out_hbm, out_ref, sems,
):
    sources = (own_ref, one_ref, two_ref, three_ref)
    both = jnp.concatenate([kron_ref[0], kron_ref[1]], axis=1)
    copies = []
    for t in range(KPAD // 8):
        stacked = jnp.concatenate(
            [
                s[KPAD * j + 8 * t : KPAD * j + 8 * t + 8, :]
                for s in sources
                for j in range(LEVELS)
            ],
            axis=0,
        )
        modal = jnp.dot(
            both, jnp.concatenate([stacked, stacked], axis=0), preferred_element_type=F32
        )
        results = [None] * LEVELS
        for a in range(ALL_LEVELS):
            scaled = modal[8 * a : 8 * a + 8] * gain_ref[a, 8 * t : 8 * t + 8, :]
            for l in range(LEVELS):
                term = coef_ref[16 * l + a : 16 * l + a + 1, :] * scaled
                results[l] = term if a == 0 else results[l] + term
        count = min(8, BLOCKS - 8 * t)
        for l in range(LEVELS):
            out_ref[pl.ds(32 * t + l, count, stride=LEVELS), :] = results[l][0:count]
        if t in OUT_TILES:
            first = 32 * (0 if not copies else OUT_TILES[len(copies) - 1] + 1)
            rows = pl.ds(first, 32 * t + 4 * count - first)
            copies.append(
                pltpu.make_async_copy(
                    out_ref.at[rows], out_hbm.at[rows], sems.at[len(copies)]
                )
            )
            copies[-1].start(priority=len(copies) % 2)
    for copy in copies:
        copy.wait()


def specs(*kinds):
    spaces = {"s": pltpu.SMEM, "v": pltpu.VMEM, "h": pltpu.HBM, "a": pl.ANY}
    return [pl.BlockSpec(memory_space=spaces[k]) for k in kinds]


def in_hbm(x):
    return pltpu.with_memory_space_constraint(x, pltpu.HBM)


def on_device(
    spectral, legendre, wave_ids, block_slot, block_start, lat_weights, drag, mode_inverse,
    level_modes, depths,
):
    lev = lax.axis_index("lev").astype(jnp.int32).reshape(1)
    spec = spectral.reshape(BLOCKS * LEVELS, 128)
    outgoing, legv, masked, pos, base = pl.pallas_call(
        forward_kernel,
        in_specs=specs("h", "h", "h", "h", "h"),
        out_specs=specs("v", "v", "v", "h", "h"),
        out_shape=(
            jax.ShapeDtypeStruct((SOURCES * SENT_ROWS, 128), BF16),
            pltpu.VMEM((BLOCKS, ROWS, LATS), BF16),
            pltpu.VMEM((BLOCKS * LEVELS, 128), F32),
            jax.ShapeDtypeStruct((BLOCKS,), jnp.int32),
            jax.ShapeDtypeStruct((BLOCKS,), jnp.int32),
        ),
        scratch_shapes=[
            pltpu.SMEM((8,), jnp.int32),
            pltpu.SMEM((BLOCKS,), jnp.int32),
            pltpu.SMEM((BLOCKS,), jnp.int32),
            pltpu.SMEM((8,), jnp.int32),
            pltpu.SMEM((BLOCKS,), jnp.int32),
            pltpu.SMEM((BLOCKS,), jnp.int32),
            pltpu.VMEM((BLOCKS // 2, 128, 128), BF16),
            pltpu.VMEM((8, 128, 128), F32),
            pltpu.VMEM((SOURCES * SENT_ROWS, 128), F32),
            pltpu.SemaphoreType.DMA((CHUNKS,)),
            pltpu.SemaphoreType.DMA((6,)),
        ],
        compiler_params=pltpu.CompilerParams(vmem_limit_bytes=24 * MB),
        name="forward",
    )(*[in_hbm(x) for x in (wave_ids, block_slot, block_start, spec, legendre)])
    pairs = SENT_ROWS // 2
    incoming = lax.all_to_all(
        outgoing.reshape(SOURCES, pairs, 2, 128), "band", split_axis=0, concat_axis=0, tiled=True
    ).reshape(SOURCES * SENT_ROWS, 128)
    filtered = pl.pallas_call(
        grid_kernel,
        in_specs=specs("v"),
        out_specs=specs("v")[0],
        out_shape=jax.ShapeDtypeStruct((SOURCES, 16, 128), BF16),
        scratch_shapes=[
            pltpu.VMEM((SOURCES * SENT_ROWS, 128), F32),
            pltpu.VMEM((4, XTILES, 256, 128), BF16),
            pltpu.VMEM((4, XTILES, 128, 128), BF16),
            pltpu.VMEM((SOURCES * 16, 128), F32),
        ],
        compiler_params=pltpu.CompilerParams(vmem_limit_bytes=16 * MB),
        name="grid",
    )(incoming)
    arrived = lax.all_to_all(filtered, "band", split_axis=0, concat_axis=0, tiled=True)
    combined = pl.pallas_call(
        direct_kernel,
        in_specs=specs("h", "h", "v", "v", "v", "v", "v"),
        out_specs=specs("v")[0],
        out_shape=jax.ShapeDtypeStruct((LEVELS * KPAD, 128), BF16),
        scratch_shapes=[
            pltpu.SMEM((BLOCKS,), jnp.int32),
            pltpu.SMEM((BLOCKS,), jnp.int32),
            pltpu.VMEM((8, 128, 128), BF16),
            pltpu.VMEM((6, 256, 128), F32),
            pltpu.VMEM((LEVELS * KPAD, 128), F32),
            pltpu.VMEM((4, 2, LATS, 128), BF16),
            pltpu.SemaphoreType.DMA((2,)),
        ],
        compiler_params=pltpu.CompilerParams(vmem_limit_bytes=16 * MB),
        name="direct",
    )(pos, base, arrived, lat_weights.reshape(1, LATS), drag, masked, legv)
    others = [
        lax.ppermute(combined, "lev", [(i, (i + s) % 4) for i in range(4)]) for s in (1, 2, 3)
    ]
    late_base, combined = lax.optimization_barrier((base, combined))
    gain, kron, coef = pl.pallas_call(
        prepare_kernel,
        in_specs=specs("s", "s", "s", "s", "v"),
        out_specs=specs("v", "v", "v"),
        out_shape=(
            pltpu.VMEM((ALL_LEVELS, KPAD, 128), F32),
            pltpu.VMEM((2, 128, 128), BF16),
            pltpu.VMEM((LEVELS * ALL_LEVELS, 128), F32),
        ),
        scratch_shapes=[pltpu.VMEM((KPAD, 128), F32)],
        compiler_params=pltpu.CompilerParams(vmem_limit_bytes=24 * MB),
        name="prepare",
    )(lev, late_base, level_modes, depths, mode_inverse)
    result = pl.pallas_call(
        vertical_kernel,
        in_specs=specs("v", "v", "v", "v", "v", "v", "v"),
        out_specs=specs("h")[0],
        out_shape=jax.ShapeDtypeStruct((BLOCKS * LEVELS, 128), F32),
        scratch_shapes=[
            pltpu.VMEM((BLOCKS * LEVELS, 128), F32),
            pltpu.SemaphoreType.DMA((len(OUT_TILES),)),
        ],
        compiler_params=pltpu.CompilerParams(vmem_limit_bytes=16 * MB),
        name="vertical",
    )(combined, *others, gain, kron, coef)
    return result.reshape(BLOCKS, LEVELS, 128)


def solution(mesh):
    placed = (
        P("band", "lev", None),
        P("band", None, None),
        P("band"),
        P("band"),
        P("band"),
        P(),
        P("lev", None, None),
        P(),
        P(),
        P(),
    )
    return jax.shard_map(
        on_device, mesh=mesh, in_specs=placed, out_specs=P("band", "lev", None), check_vma=False
    )
```
